256 devices in a mesh: slab: 16 (over y, z_hi), col: 16 (over x, z_lo, core).
Axes of the slice: x: 4, y: 4, z: 8 (z_hi: 4, z_lo: 2; z = z_hi * 2 + z_lo), core: 2. Of those that a mesh axis runs over, the one named last changes fastest.
Arguments:
- pressure: float32 [256, 1024, 128], P('slab', 'col'), may hold values from -6 to 6
- source: float32 [256, 1024, 128], P('slab', 'col'), may hold values from -12 to 12
- accum: float32 [256, 1024, 128], P('slab', 'col'), may hold values from 0.2 to 2
- trans_z: float32 [256, 1024, 128], P('slab', 'col'), may hold values from 0.1 to 10
- trans_x: float32 [256, 1024, 128], P('slab', 'col'), may hold values from 0.1 to 10
- trans_y: float32 [256, 1024, 128], P('slab', 'col'), may hold values from 0.1 to 10
- nnc_cell: int32 [16, 16, 16, 128], P('slab', 'col'), may hold values from 0 to 1023, as said below
- nnc_trans: float32 [16, 16, 16, 128, 128], P('slab', 'col'), may hold values from 0 to 4, as said below
- fault_cell: int32 [16, 16, 16, 128], P('slab', 'col'), may hold values from -1 to 131071, as said below
- base_stress: float32 [16, 3, 32768], P('slab', None, 'col'), may hold values from -6 to 6
- slip_start: float32 [16, 3, 32768], P('slab', None, 'col'), may hold values from -4 to 4
- stiff_diag: float32 [16, 32768], P('slab', 'col'), may hold values from 1 to 6
- active_set: int32 [2, 16, 32768], P(None, 'slab', 'col'), may hold values 0 or 1
- mortar_blocks: bfloat16 [16, 256, 4, 128, 128], P('slab', 'col'), may hold values from -0.25 to 0.25
- mortar_cols: int32 [16, 256, 4], P('slab', 'col'), may hold values from 0 to 255
Outputs:
- pressure_out: float32 [256, 1024, 128], P('slab', 'col')
- slip: float32 [16, 3, 32768], P('slab', None, 'col')
- traction: float32 [16, 3, 32768], P('slab', None, 'col')
The draws below stay inside these ranges and needn't reach their ends.
Inputs may be any that keep to these rules, and one draw needn't show every extreme that they name: `nnc_cell`: A slot whose nnc_trans is 0 on its whole line is empty and its line is 0. No slot joins a slab to itself; between slabs 0 and 1 all 128 slots of every column are live. nnc_trans[s, c, q, k, y] equals nnc_trans[q, c, s, k, y]; on live slots every entry lies between 0.1 and 4. `fault_cell`: -1 marks an empty slot; the live slots of each (s, c, o) come first. In each slab one owner gets all 128 slots live from every source column.
All inputs are finite; a program needn't handle non-finite values. No bound on the sum of `active_set` on one device may be relied on, other than what follows from the above.
Results may differ from the reference program's by a relative error of at most 0.0017.
Values may be sent and summed in bfloat16 or wider, within the bound.
No kernel may reach another device: no remote copies, remote signals or barrier semaphores. Data moves between devices by JAX's collectives and lax.ppermute only.
A program may use at most 64 MiB of HBM per device.

```python
import math
import jax
import jax.numpy as jnp
from jax import lax

CZ = 16
CX = 64
NY = 128
CAP = 128
FCAP = 128
TILE = 128
NB = 4
ITERS_FLOW = 3
ITERS_C = 2
NZ = 256
NX = 1024
CELLS_DEV = 131072
F_TOT = 32768
TILES = 256
N_SLAB = 16
N_COL = 16


def nnc_live(key):
    raw = jax.random.randint(jax.random.fold_in(key, 11), (N_SLAB, N_SLAB, N_COL), CAP // 4, CAP + 1)
    lower = jnp.arange(N_SLAB)[:, None, None]
    upper = jnp.arange(N_SLAB)[None, :, None]
    counts = jnp.where(lower < upper, raw, jnp.transpose(raw, (1, 0, 2)))
    pinned = (lower == 0) & (upper == 1) | (lower == 1) & (upper == 0)
    counts = jnp.where(pinned, CAP, counts)
    counts = jnp.where(lower == upper, 0, counts)
    counts = jnp.transpose(counts, (0, 2, 1))
    return jnp.arange(CAP)[None, None, None, :] < counts[..., None]


def draw_nnc_cell(key, part):
    live = nnc_live(key)
    cells = jax.random.randint(jax.random.fold_in(key, 13), (N_SLAB, N_COL, N_SLAB, CAP), 0, CZ * CX)
    return jnp.where(live, cells, 0).astype(jnp.int32)


def draw_nnc_trans(key, part):
    live = nnc_live(key)
    shape = (N_SLAB, N_SLAB, N_COL, CAP, NY)
    noise = jax.random.uniform(jax.random.fold_in(key, 17), shape, jnp.float32)
    raw = jnp.exp(math.log(0.1) + (math.log(4.0) - math.log(0.1)) * noise)
    lower = jnp.arange(N_SLAB)[:, None, None, None, None]
    upper = jnp.arange(N_SLAB)[None, :, None, None, None]
    paired = jnp.where(lower < upper, raw, jnp.transpose(raw, (1, 0, 2, 3, 4)))
    paired = jnp.transpose(paired, (0, 2, 1, 3, 4))
    return jnp.where(live[..., None], paired, 0.0).astype(jnp.float32)


def draw_fault_cell(key, part):
    hot = jax.random.randint(jax.random.fold_in(key, 21), (N_SLAB,), 0, N_COL)
    counts = jax.random.randint(jax.random.fold_in(key, 22), (N_SLAB, N_COL, N_COL), max(1, FCAP // 8), FCAP // 2 + 1)
    owner = jnp.arange(N_COL)[None, None, :]
    counts = jnp.where(owner == hot[:, None, None], FCAP, counts)
    cells = jax.random.randint(jax.random.fold_in(key, 23), (N_SLAB, N_COL, N_COL, FCAP), 0, CELLS_DEV)
    live = jnp.arange(FCAP)[None, None, None, :] < counts[..., None]
    return jnp.where(live, cells, -1).astype(jnp.int32)


def plant(values, stream_key, least, high):
    longest = values.shape.index(max(values.shape))
    spots = []
    for shift in (0, 1):
        where = [jax.random.randint(jax.random.fold_in(stream_key, axis), (), 0, length) for axis, length in enumerate(values.shape)]
        where[longest] = (where[longest] + shift) % values.shape[longest]
        spots.append(tuple(where))
    return values.at[spots[0]].set(least).at[spots[1]].set(high)


def steps_of(rng, dims, pieces, least, high):
    factor_of = 1.0
    for dim, shards_of in pieces:
        draws = jax.random.uniform(jax.random.fold_in(jax.random.fold_in(rng, 6), dim), (shards_of,), jnp.float32, least / len(pieces), high / len(pieces))
        factor_of = factor_of * jnp.repeat(jnp.exp(draws), dims[dim] // shards_of).reshape((-1,) + (1,) * (len(dims) - 1 - dim))
    return factor_of


def centred(own_key, shape, width, limit, pieces=(), held_as=jnp.bfloat16):
    result = width * jax.random.normal(own_key, shape, jnp.float32)
    if pieces:
        result = result * steps_of(own_key, shape, pieces, -0.22, 0.18)
    return jnp.clip(result, -limit, limit).astype(held_as)


def setup_inputs(seed: int = 0) -> dict:
    arg_keys = jax.random.split(jax.random.key(seed), 16)
    pressure = centred(arg_keys[0], (NZ, NX, NY), 1.0, 6.0, ((0, 16), (1, 16)), jnp.float32)
    source = centred(arg_keys[1], (NZ, NX, NY), 2.0, 12.0, ((0, 16), (1, 16)), jnp.float32)
    accum = jnp.clip(jnp.exp(math.log(2.0) - 2.3025851 * jax.random.uniform(arg_keys[2], (NZ, NX, NY), jnp.float32) ** steps_of(arg_keys[2], (NZ, NX, NY), ((0, 16), (1, 16)), -0.2, 0.2)), 0.2, 2.0)
    trans_z = jnp.clip(jnp.exp(math.log(10.0) - 4.6051702 * jax.random.uniform(arg_keys[3], (NZ, NX, NY), jnp.float32) ** steps_of(arg_keys[3], (NZ, NX, NY), ((0, 16), (1, 16)), -0.2, 0.2)), 0.1, 10.0)
    trans_x = jnp.clip(jnp.exp(math.log(10.0) - 4.6051702 * jax.random.uniform(arg_keys[4], (NZ, NX, NY), jnp.float32) ** steps_of(arg_keys[4], (NZ, NX, NY), ((0, 16), (1, 16)), -0.2, 0.2)), 0.1, 10.0)
    trans_y = jnp.clip(jnp.exp(math.log(10.0) - 4.6051702 * jax.random.uniform(arg_keys[5], (NZ, NX, NY), jnp.float32) ** steps_of(arg_keys[5], (NZ, NX, NY), ((0, 16), (1, 16)), -0.2, 0.2)), 0.1, 10.0)
    nnc_cell = draw_nnc_cell(jax.random.fold_in(arg_keys[15], 71), 0)
    nnc_trans = draw_nnc_trans(jax.random.fold_in(arg_keys[15], 71), 0)
    fault_cell = draw_fault_cell(jax.random.fold_in(arg_keys[15], 71), 0)
    base_stress = centred(arg_keys[9], (N_SLAB, 3, F_TOT), 1.0, 6.0, ((0, 16), (2, 16)), jnp.float32)
    slip_start = centred(arg_keys[10], (N_SLAB, 3, F_TOT), 0.5, 4.0, ((0, 16), (2, 16)), jnp.float32)
    stiff_diag = jnp.clip(jnp.exp(math.log(6.0) - 1.7917595 * jax.random.uniform(arg_keys[11], (N_SLAB, F_TOT), jnp.float32) ** steps_of(arg_keys[11], (N_SLAB, F_TOT), ((0, 16), (1, 16)), -0.2, 0.2)), 1.0, 6.0)
    active_set = plant((jax.random.randint(arg_keys[12], (ITERS_C, N_SLAB, F_TOT), 0, 3) < 2).astype(jnp.int32), jax.random.fold_in(arg_keys[12], 1), 0, 1)
    mortar_blocks = centred(arg_keys[13], (N_SLAB, TILES, NB, TILE, TILE), (TILE * NB) ** -0.5, 0.25, ((0, 16), (1, 16)))
    mortar_cols = plant(jax.random.randint(arg_keys[14], (N_SLAB, TILES, NB), 0, TILES), jax.random.fold_in(arg_keys[14], 1), 0, TILES - 1).astype(jnp.int32)
    return {"pressure": pressure, "source": source, "accum": accum, "trans_z": trans_z, "trans_x": trans_x, "trans_y": trans_y, "nnc_cell": nnc_cell, "nnc_trans": nnc_trans, "fault_cell": fault_cell, "base_stress": base_stress, "slip_start": slip_start, "stiff_diag": stiff_diag, "active_set": active_set, "mortar_blocks": mortar_blocks, "mortar_cols": mortar_cols}


BIOT = 0.8


def global_cell(local, slab_index, col_index):
    depth = slab_index * CZ + local // (CX * NY)
    across = col_index * CX + (local // NY) % CX
    along = local % NY
    return ((depth * NX + across) * NY + along).astype(jnp.int32)


def global_line(local, slab_index, col_index):
    depth = slab_index * CZ + local // CX
    across = col_index * CX + local % CX
    return (depth * NX + across).astype(jnp.int32)


def lower_face(face, axis):
    shape = list(face.shape)
    shape[axis] = 1
    zero_layer = jnp.zeros(shape, jnp.float32)
    kept = lax.slice_in_dim(face, 0, face.shape[axis] - 1, axis=axis)
    upper = jnp.concatenate([kept, zero_layer], axis)
    below = jnp.concatenate([zero_layer, kept], axis)
    return upper, below


def shifted(field, axis):
    shape = list(field.shape)
    shape[axis] = 1
    zero_layer = jnp.zeros(shape, jnp.float32)
    count = field.shape[axis]
    after = jnp.concatenate([lax.slice_in_dim(field, 1, count, axis=axis), zero_layer], axis)
    before = jnp.concatenate([zero_layer, lax.slice_in_dim(field, 0, count - 1, axis=axis)], axis)
    return after, before


def stiffness(slip_half, blocks, columns):
    tiles = slip_half.reshape(3, TILES, TILE)
    picked = tiles[:, columns]
    coupled = jnp.einsum("rbij,crbj->cri", blocks.astype(jnp.float32), picked.astype(jnp.float32))
    return coupled.reshape(3, F_TOT)


def reference(pressure, source, accum, trans_z, trans_x, trans_y, nnc_cell, nnc_trans, fault_cell, base_stress, slip_start, stiff_diag, active_set, mortar_blocks, mortar_cols):
    total_cells = NZ * NX * NY
    total_lines = NZ * NX
    face_z, below_z = lower_face(trans_z, 0)
    face_x, below_x = lower_face(trans_x, 1)
    face_y, below_y = lower_face(trans_y, 2)
    slab_index = jnp.arange(N_SLAB, dtype=jnp.int32)[:, None, None, None]
    col_index = jnp.arange(N_COL, dtype=jnp.int32)[None, :, None, None]
    near = global_line(nnc_cell, slab_index, col_index)
    far = jnp.transpose(near, (2, 1, 0, 3)).ravel()
    near = near.ravel()
    conduct = nnc_trans.reshape(-1, NY)
    nnc_diagonal = jax.ops.segment_sum(conduct, near, total_lines).reshape(pressure.shape)
    diagonal = accum + face_z + below_z + face_x + below_x + face_y + below_y + nnc_diagonal
    field = pressure
    for sweep in range(ITERS_FLOW):
        after_z, before_z = shifted(field, 0)
        after_x, before_x = shifted(field, 1)
        after_y, before_y = shifted(field, 2)
        neighbours = face_z * after_z + below_z * before_z + face_x * after_x + below_x * before_x
        neighbours = neighbours + face_y * after_y + below_y * before_y
        lines = field.reshape(total_lines, NY)
        linked = jax.ops.segment_sum(conduct * lines[far], near, total_lines).reshape(field.shape)
        field = (source + neighbours + linked) / diagonal
    valid = fault_cell >= 0
    safe = jnp.maximum(fault_cell, 0)
    fault_global = global_cell(safe, slab_index, col_index)
    fault_press = jnp.where(valid, field.ravel()[fault_global], 0.0)
    fault_press = jnp.transpose(fault_press, (0, 2, 1, 3)).reshape(N_SLAB, F_TOT)
    load = jnp.concatenate([base_stress[:, :1] - BIOT * fault_press[:, None], base_stress[:, 1:]], 1)
    slip = slip_start
    traction = load
    for turn in range(ITERS_C):
        slip_half = slip.astype(jnp.bfloat16)
        coupled = lax.map(lambda group: stiffness(group[0], group[1], group[2]), (slip_half, mortar_blocks, mortar_cols))
        traction = load - coupled
        slip = slip + active_set[turn].astype(jnp.float32)[:, None, :] * traction / stiff_diag[:, None, :]
    normal = traction[:, 0].reshape(N_SLAB, N_COL, N_COL, FCAP)
    normal = jnp.transpose(normal, (0, 2, 1, 3))
    returned = jax.ops.segment_sum(jnp.where(valid, normal, 0.0).ravel(), fault_global.ravel(), total_cells)
    pressure_out = field + returned.reshape(field.shape) / diagonal
    return pressure_out, slip, traction
```

```python
import functools

import jax
import jax.numpy as jnp
from jax import lax
from jax.experimental import pallas as pl
from jax.experimental.pallas import tpu as pltpu
from jax.sharding import PartitionSpec as P

ITERS_FLOW = 3
BIOT = 0.8
F32 = jnp.float32
BF16 = jnp.bfloat16
NT = (((1,), (1,)), ((), ()))


def call(body, outs, *args, smem=(), scratch=(), mib=40):
    ins = [
        pl.BlockSpec(memory_space=pltpu.SMEM if i in smem else pltpu.VMEM)
        for i in range(len(args))
    ]
    return pl.pallas_call(
        body,
        in_specs=ins,
        out_specs=[pl.BlockSpec(memory_space=pltpu.VMEM) for _ in outs],
        out_shape=[jax.ShapeDtypeStruct(s, d) for s, d in outs],
        scratch_shapes=list(scratch),
        compiler_params=pltpu.CompilerParams(vmem_limit_bytes=mib << 20),
    )(*args)


def iota(shape, dim):
    return lax.broadcasted_iota(jnp.int32, shape, dim)


def halves(x):
    high = x.astype(BF16)
    return high, (x - high.astype(F32)).astype(BF16)


def fill_hot(hot_ref, lines):
    rows = hot_ref.shape[0]
    ids = iota((rows, 128), 0)
    for q in range(lines.shape[0]):
        hit = ids == lines[q : q + 1, :]
        hot_ref[:, q * 128 : (q + 1) * 128] = jnp.where(hit, 1.0, 0.0).astype(BF16)


def gather_lines(hot_ref, field, out_ref):
    turned = field.T.astype(BF16)
    for q in range(0, out_ref.shape[0], 2):
        got = jnp.dot(
            turned, hot_ref[:, q * 128 : (q + 2) * 128], preferred_element_type=F32
        ).astype(BF16)
        out_ref[q] = got[:, :128]
        out_ref[q + 1] = got[:, 128:]


def scatter_lines(hot_ref, values_ref):
    both = lax.dot_general(hot_ref[...], values_ref[...], NT, preferred_element_type=F32)
    return both[:, :128] + both[:, 128:]


def put_halves(values_ref, q, values):
    high, low = halves(values)
    values_ref[:128, q * 128 : (q + 1) * 128] = high
    values_ref[128:, q * 128 : (q + 1) * 128] = low


def first_kernel(field_ref, cell_ref, hot_ref, out_ref):
    depth, width, lateral = field_ref.shape
    fill_hot(hot_ref, cell_ref[...])
    gather_lines(hot_ref, field_ref[...].reshape(depth * width, lateral), out_ref)


def edges_kernel(
    field_ref, face_z_ref, face_x_ref, up_ref, down_ref, right_ref, left_ref
):
    depth, width, _ = field_ref.shape
    up_ref[0] = field_ref[depth - 1]
    up_ref[1] = face_z_ref[depth - 1]
    down_ref[...] = field_ref[0]
    for i in range(depth):
        right_ref[0, i : i + 1, :] = field_ref[i, width - 1 : width, :]
        right_ref[1, i : i + 1, :] = face_x_ref[i, width - 1 : width, :]
        left_ref[i : i + 1, :] = field_ref[i, 0:1, :]


def setup_kernel(
    ends_ref,
    accum_ref,
    face_z_ref,
    face_x_ref,
    face_y_ref,
    hot_ref,
    conduct_ref,
    fault_ref,
    turned_ref,
    partial_ref,
    fault_hot_ref,
    values_ref,
):
    depth, width, lateral = accum_ref.shape
    for q in range(conduct_ref.shape[0]):
        turned = conduct_ref[q].T
        turned_ref[q] = turned
        put_halves(values_ref, q, turned)
    linked = scatter_lines(hot_ref, values_ref)
    last_z = ends_ref[0] != 0
    last_x = ends_ref[1] != 0
    across = iota((width, lateral), 0)
    along = iota((width, lateral), 1)
    for i in range(depth):
        total = accum_ref[i] + linked[i * width : (i + 1) * width]
        own_z = face_z_ref[i]
        if i == depth - 1:
            own_z = jnp.where(last_z, 0.0, own_z)
        total = total + own_z
        if i > 0:
            total = total + face_z_ref[i - 1]
        own_x = face_x_ref[i]
        total = total + jnp.where((across == width - 1) & last_x, 0.0, own_x)
        total = total + jnp.where(across == 0, 0.0, pltpu.roll(own_x, 1, 0))
        own_y = jnp.where(along == lateral - 1, 0.0, face_y_ref[i])
        partial_ref[i] = total + own_y + pltpu.roll(own_y, 1, 1)
    fill_hot(fault_hot_ref, fault_ref[...] >> 7)


def sweep_kernel(
    first,
    last,
    incoming_ref,
    turned_ref,
    hot_ref,
    field_ref,
    source_ref,
    diag_ref,
    face_z_ref,
    face_x_ref,
    face_y_ref,
    below_ref,
    above_ref,
    behind_ref,
    ahead_ref,
    lower_z_ref,
    lower_x_ref,
    *refs,
):
    depth, width, lateral = field_ref.shape
    refs = list(refs)
    values_ref = refs.pop()
    fault_ref, fault_hot_ref = (refs.pop(0), refs.pop(0)) if last else (None, None)
    new_ref = refs.pop(0)
    inverse_ref = refs.pop(0) if first else diag_ref
    for q in range(incoming_ref.shape[0]):
        put_halves(values_ref, q, turned_ref[q] * incoming_ref[q].astype(F32))
    linked = scatter_lines(hot_ref, values_ref)
    across = iota((width, lateral), 0)
    along = iota((width, lateral), 1)
    for i in range(depth):
        field = field_ref[i]
        face_z = face_z_ref[i]
        lower_z = face_z_ref[i - 1] if i > 0 else lower_z_ref[...]
        above = field_ref[i + 1] if i < depth - 1 else above_ref[...]
        below = field_ref[i - 1] if i > 0 else below_ref[...]
        total = source_ref[i] + linked[i * width : (i + 1) * width]
        total = total + face_z * above + lower_z * below
        face_x = face_x_ref[i]
        lower_x = lower_x_ref[i : i + 1, :]
        ahead = jnp.where(
            across == width - 1, ahead_ref[i : i + 1, :], pltpu.roll(field, width - 1, 0)
        )
        flow = jnp.where(
            across == 0,
            lower_x * behind_ref[i : i + 1, :],
            pltpu.roll(face_x * field, 1, 0),
        )
        total = total + face_x * ahead + flow
        face_y = jnp.where(along == lateral - 1, 0.0, face_y_ref[i])
        total = total + face_y * pltpu.roll(field, lateral - 1, 1)
        total = total + pltpu.roll(face_y * field, 1, 1)
        if first:
            whole = diag_ref[i] + jnp.where(across == 0, lower_x, 0.0)
            if i == 0:
                whole = whole + lower_z
            inverse = 1.0 / whole
            inverse_ref[i] = inverse
        else:
            inverse = diag_ref[i]
        new_ref[i] = total * inverse
    lines = new_ref[...].reshape(depth * width, lateral)
    if last:
        (press_ref,) = refs
        high, low = halves(lines.T)
        both = jnp.concatenate([high, low], 0)
        side = iota((lateral, 128), 0)
        for q in range(fault_ref.shape[0]):
            got = jnp.dot(
                both, fault_hot_ref[:, q * 128 : (q + 1) * 128], preferred_element_type=F32
            )
            got = got[:lateral] + got[lateral:]
            lane = fault_ref[q : q + 1, :] & 127
            got = jnp.sum(jnp.where(side == lane, got, 0.0), 0, keepdims=True)
            press_ref[0, q : q + 1, :] = got
        mine = press_ref[0]
        for o in range(1, press_ref.shape[0]):
            press_ref[o] = mine
    else:
        out_ref, up_ref, down_ref, right_ref, left_ref = refs
        gather_lines(hot_ref, lines, out_ref)
        up_ref[...] = new_ref[depth - 1]
        down_ref[...] = new_ref[0]
        for i in range(depth):
            right_ref[i : i + 1, :] = new_ref[i, width - 1 : width, :]
            left_ref[i : i + 1, :] = new_ref[i, 0:1, :]


def couple(select, tiles, blocks_ref):
    rows, per = blocks_ref.shape[:2]
    picked = [jnp.dot(select, t, preferred_element_type=F32) for t in tiles]
    ids = iota((rows, 128), 0)
    total = None
    for r in range(rows):
        for b in range(per):
            n = r * per + b
            left = [jnp.where(ids == r, p[n : n + 1, :], 0.0) for p in picked]
            left = (jnp.concatenate(left, 0) if len(left) > 1 else left[0]).astype(BF16)
            part = lax.dot_general(left, blocks_ref[r, b], NT, preferred_element_type=F32)
            total = part if total is None else total + part
    return total


def contact_one_kernel(
    whole_ref,
    cols_ref,
    blocks_ref,
    base_ref,
    slip_ref,
    stiff_ref,
    active_ref,
    packed_ref,
    own_ref,
):
    owners = whole_ref.shape[0]
    rows = base_ref.shape[1]
    ids = owners * rows
    select = jnp.where(iota((cols_ref.shape[0], ids), 1) == cols_ref[...], 1.0, 0.0)
    tiles = [
        whole_ref[:, p * rows : (p + 1) * rows, :].reshape(ids, 128) for p in range(3)
    ]
    coupled = couple(select.astype(BF16), tiles, blocks_ref)
    gain = active_ref[...].astype(F32) / stiff_ref[...]
    parts = [
        slip_ref[p] + gain * (base_ref[p] - coupled[p * rows : (p + 1) * rows])
        for p in range(3)
    ]
    mine = jnp.concatenate([parts[0], -BIOT * gain, parts[1], parts[2]], 0)
    own_ref[...] = mine
    for o in range(owners):
        packed_ref[o] = mine


def contact_two_kernel(
    whole_ref, cols_ref, blocks_ref, base_ref, own_ref, stiff_ref, active_ref, done_ref
):
    owners = whole_ref.shape[0]
    rows = base_ref.shape[1]
    ids = owners * rows
    select = jnp.where(iota((cols_ref.shape[0], ids), 1) == cols_ref[...], 1.0, 0.0)
    tiles = [
        whole_ref[:, p * rows : (p + 1) * rows, :].reshape(ids, 128).astype(BF16)
        for p in (2, 3)
    ]
    coupled = couple(select.astype(BF16), tiles, blocks_ref)
    gain = active_ref[...].astype(F32) / stiff_ref[...]
    for p in (1, 2):
        traction = base_ref[p] - coupled[(p - 1) * rows : p * rows]
        done_ref[p - 1] = own_ref[(p + 1) * rows : (p + 2) * rows] + gain * traction
        done_ref[p + 1] = traction


def tail_kernel(
    me_ref,
    press_ref,
    slope_ref,
    cols_ref,
    blocks_ref,
    base_ref,
    own_ref,
    stiff_ref,
    active_ref,
    done_ref,
    normal_ref,
    slip_ref,
    traction_ref,
):
    sources, owners, _ = press_ref.shape
    rows = base_ref.shape[1]
    ids = sources * owners
    press = press_ref[...]
    slips = slope_ref[0] + slope_ref[1] * press
    select = jnp.where(iota((cols_ref.shape[0], ids), 1) == cols_ref[...], 1.0, 0.0)
    tiles = [slips.reshape(ids, 128).astype(BF16)]
    coupled = couple(select.astype(BF16), tiles, blocks_ref)
    mine = jnp.where(iota(press.shape, 1) == me_ref[0], press, 0.0)
    mine = jnp.sum(mine, 1)
    slip = own_ref[:rows] + own_ref[rows : 2 * rows] * mine
    traction = base_ref[0] - BIOT * mine - coupled
    normal_ref[...] = traction
    traction_ref[0] = traction
    slip_ref[0] = slip + active_ref[...].astype(F32) / stiff_ref[...] * traction
    for p in (1, 2):
        slip_ref[p] = done_ref[p - 1]
        traction_ref[p] = done_ref[p + 1]


def back_kernel(
    normal_ref, fault_ref, fault_hot_ref, field_ref, inverse_ref, out_ref, values_ref
):
    depth, width, lateral = field_ref.shape
    side = iota((lateral, 128), 0)
    for q in range(normal_ref.shape[0]):
        lane = fault_ref[q : q + 1, :] & 127
        put_halves(values_ref, q, jnp.where(side == lane, normal_ref[q : q + 1, :], 0.0))
    returned = scatter_lines(fault_hot_ref, values_ref).reshape(depth, width, lateral)
    out_ref[...] = field_ref[...] + returned * inverse_ref[...]


def shift(block, axis, step):
    count = lax.axis_size(axis)
    route = [(i, i + step) for i in range(count) if 0 <= i + step < count]
    return lax.ppermute(block, axis, route)


def swap(blocks, axis):
    return lax.all_to_all(blocks, axis, split_axis=0, concat_axis=0, tiled=True)


def per_device(
    pressure,
    source,
    accum,
    trans_z,
    trans_x,
    trans_y,
    nnc_cell,
    nnc_trans,
    fault_cell,
    base_stress,
    slip_start,
    stiff_diag,
    active_set,
    mortar_blocks,
    mortar_cols,
):
    depth, width, lateral = pressure.shape
    slabs = lax.axis_size("slab")
    columns = lax.axis_size("col")
    lines = depth * width
    grid = ((depth, width, lateral), F32)
    slots = slabs * 128
    nodes = columns * 128
    rows = mortar_blocks.shape[1]
    cells = nnc_cell[0, 0]
    faults = fault_cell[0, 0]
    blocks = mortar_blocks[0]
    tile_cols = mortar_cols[0].reshape(-1, 1)
    turned_cols = tile_cols % columns * columns + tile_cols // columns
    base = base_stress[0].reshape(3, rows, 128)
    slip0 = slip_start[0].reshape(3, rows, 128)
    stiff = stiff_diag[0].reshape(rows, 128)
    active = active_set[:, 0].reshape(-1, rows, 128)
    me = lax.axis_index("col")
    last_z = lax.axis_index("slab") == slabs - 1
    ends = jnp.stack([last_z, me == columns - 1]).astype(jnp.int32)
    whole_values = pltpu.VMEM((2 * lateral, slots), BF16)

    layer = ((width, lateral), F32)
    wall = ((depth, lateral), F32)
    hot, outgoing = call(
        first_kernel,
        [((lines, slots), BF16), ((slabs, lateral, 128), BF16)],
        pressure,
        cells,
    )
    incoming = swap(outgoing, "slab")
    up, down, right, left = call(
        edges_kernel,
        [((2, *layer[0]), F32), layer, ((2, *wall[0]), F32), wall],
        pressure,
        trans_z,
        trans_x,
    )
    up = shift(up, "slab", 1)
    right = shift(right, "col", 1)
    below, lower_z = up[0], up[1]
    behind, lower_x = right[0], right[1]
    above = shift(down, "slab", -1)
    ahead = shift(left, "col", -1)
    turned, diag, fault_hot = call(
        setup_kernel,
        [((slabs, lateral, 128), F32), grid, ((lines, nodes), BF16)],
        ends,
        accum,
        trans_z,
        trans_x,
        trans_y,
        hot,
        nnc_trans[0, 0],
        faults,
        smem=(0,),
        scratch=(whole_values,),
    )

    slip_half = slip0.astype(BF16).reshape(1, 3 * rows, 128)
    whole = swap(jnp.broadcast_to(slip_half, (columns, 3 * rows, 128)), "col")
    packed, own = call(
        contact_one_kernel,
        [((columns, 4 * rows, 128), F32), ((4 * rows, 128), F32)],
        whole,
        tile_cols,
        blocks,
        base,
        slip0,
        stiff,
        active[0],
    )
    packed = swap(packed, "col")
    (done,) = call(
        contact_two_kernel,
        [((4, rows, 128), F32)],
        packed,
        tile_cols,
        blocks,
        base,
        own,
        stiff,
        active[1],
    )
    slope = packed[:, : 2 * rows].reshape(columns, 2, rows, 128).transpose(1, 2, 0, 3)

    field = pressure
    for sweep in range(ITERS_FLOW):
        first = sweep == 0
        last = sweep == ITERS_FLOW - 1
        extra = [faults, fault_hot] if last else []
        outs = [grid] + ([grid] if first else [])
        if last:
            outs += [((columns, columns, 128), F32)]
        else:
            outs += [((slabs, lateral, 128), BF16), layer, layer, wall, wall]
        got = list(call(
            functools.partial(sweep_kernel, first, last),
            outs,
            incoming,
            turned,
            hot,
            field,
            source,
            diag,
            trans_z,
            trans_x,
            trans_y,
            below,
            above,
            behind,
            ahead,
            lower_z,
            lower_x,
            *extra,
            scratch=(whole_values,),
        ))
        field = got.pop(0)
        if first:
            diag = got.pop(0)
        if not last:
            incoming = swap(got[0], "slab")
            below = shift(got[1], "slab", 1)
            behind = shift(got[3], "col", 1)
            above = shift(got[2], "slab", -1)
            ahead = shift(got[4], "col", -1)
    press = swap(got[0], "col")
    normal, slip, traction = call(
        tail_kernel,
        [((rows, 128), F32), ((3, rows, 128), F32), ((3, rows, 128), F32)],
        me.reshape(1).astype(jnp.int32),
        press,
        slope,
        turned_cols,
        blocks,
        base,
        own,
        stiff,
        active[1],
        done,
        smem=(0,),
    )
    normal = swap(normal.reshape(columns, -1, 128), "col").reshape(columns, 128)
    (pressure_out,) = call(
        back_kernel,
        [grid],
        normal,
        faults,
        fault_hot,
        field,
        diag,
        scratch=(pltpu.VMEM((2 * lateral, nodes), BF16),),
    )
    return (pressure_out, slip.reshape(1, 3, -1), traction.reshape(1, 3, -1))


def solution(mesh):
    return jax.shard_map(
        per_device,
        mesh=mesh,
        in_specs=(
            P("slab", "col", None),
            P("slab", "col", None),
            P("slab", "col", None),
            P("slab", "col", None),
            P("slab", "col", None),
            P("slab", "col", None),
            P("slab", "col", None, None),
            P("slab", "col", None, None, None),
            P("slab", "col", None, None),
            P("slab", None, "col"),
            P("slab", None, "col"),
            P("slab", "col"),
            P(None, "slab", "col"),
            P("slab", "col", None, None, None),
            P("slab", "col", None),
        ),
        out_specs=(P("slab", "col", None), P("slab", None, "col"), P("slab", None, "col")),
        check_vma=False,
    )
```

```python
import functools

import jax
import jax.numpy as jnp
from jax import lax
from jax.experimental import pallas as pl
from jax.experimental.pallas import tpu as pltpu
from jax.sharding import PartitionSpec as P

ITERS_FLOW = 3
BIOT = 0.8
F32 = jnp.float32
BF16 = jnp.bfloat16
NT = (((1,), (1,)), ((), ()))


def call(body, outs, *args, smem=(), hbm=(), scratch=(), mib=14):
    spaces = [
        pltpu.SMEM if i in smem else pltpu.HBM if i in hbm else pltpu.VMEM
        for i in range(len(args))
    ]
    args = [
        pltpu.with_memory_space_constraint(a, pltpu.HBM) if i in hbm else a
        for i, a in enumerate(args)
    ]
    far = [len(o) > 2 for o in outs]
    return pl.pallas_call(
        body,
        in_specs=[pl.BlockSpec(memory_space=space) for space in spaces],
        out_specs=[
            pl.BlockSpec(memory_space=pltpu.HBM if f else pltpu.VMEM) for f in far
        ],
        out_shape=[
            pltpu.HBM(*o[:2]) if f else jax.ShapeDtypeStruct(*o)
            for o, f in zip(outs, far)
        ],
        scratch_shapes=list(scratch),
        compiler_params=pltpu.CompilerParams(vmem_limit_bytes=mib << 20),
    )(*args)


def begin(pairs, sems, at=0):
    copies = [
        pltpu.make_async_copy(source, target, sems.at[at + i])
        for i, (source, target) in enumerate(pairs)
    ]
    for copy in copies:
        copy.start()
    return copies


def finish(copies):
    for copy in copies:
        copy.wait()


def iota(shape, dim):
    return lax.broadcasted_iota(jnp.int32, shape, dim)


def halves(x):
    high = x.astype(BF16)
    return high, (x - high.astype(F32)).astype(BF16)


def fill_hot(hot_ref, lines):
    rows = hot_ref.shape[0]
    ids = iota((rows, 128), 0)
    for q in range(lines.shape[0]):
        hit = ids == lines[q : q + 1, :]
        hot_ref[:, q * 128 : (q + 1) * 128] = jnp.where(hit, 1.0, 0.0).astype(BF16)


def gather_lines(hot_ref, field, out_ref):
    turned = field.T.astype(BF16)
    for q in range(0, out_ref.shape[0], 2):
        got = jnp.dot(
            turned, hot_ref[:, q * 128 : (q + 2) * 128], preferred_element_type=F32
        ).astype(BF16)
        out_ref[q] = got[:, :128]
        out_ref[q + 1] = got[:, 128:]


def scatter_lines(hot_ref, values_ref):
    both = lax.dot_general(hot_ref[...], values_ref[...], NT, preferred_element_type=F32)
    return both[:, :128] + both[:, 128:]


def put_halves(values_ref, q, values):
    high, low = halves(values)
    values_ref[:128, q * 128 : (q + 1) * 128] = high
    values_ref[128:, q * 128 : (q + 1) * 128] = low


def ready_kernel(slip_ref, out_ref):
    parts, rows, _ = slip_ref.shape
    for p in range(parts):
        out_ref[0, p * rows : (p + 1) * rows, :] = slip_ref[p].astype(BF16)
    mine = out_ref[0]
    for o in range(1, out_ref.shape[0]):
        out_ref[o] = mine


def first_kernel(
    field_hbm,
    face_z_hbm,
    face_x_hbm,
    cell_ref,
    out_hbm,
    up_ref,
    down_ref,
    right_ref,
    left_ref,
    hot_ref,
    field_ref,
    wall_ref,
    out_ref,
    sems,
):
    depth, width, lateral = field_ref.shape
    reads = begin(
        [
            (field_hbm, field_ref),
            (face_z_hbm.at[depth - 1], up_ref.at[1]),
            (face_x_hbm.at[:, pl.ds(width - 8, 8), :], wall_ref),
        ],
        sems,
    )
    fill_hot(hot_ref, cell_ref[...])
    finish(reads)
    gather_lines(hot_ref, field_ref[...].reshape(depth * width, lateral), out_ref)
    writes = begin([(out_ref, out_hbm)], sems, 3)
    up_ref[0] = field_ref[depth - 1]
    down_ref[...] = field_ref[0]
    for i in range(depth):
        right_ref[0, i : i + 1, :] = field_ref[i, width - 1 : width, :]
        right_ref[1, i : i + 1, :] = wall_ref[i, 7:8, :]
        left_ref[i : i + 1, :] = field_ref[i, 0:1, :]
    finish(writes)


def sweep_kernel(
    first,
    last,
    incoming_ref,
    turned_hbm,
    field_hbm,
    source_hbm,
    face_z_hbm,
    face_x_hbm,
    face_y_hbm,
    diag_hbm,
    cell_ref,
    below_ref,
    above_ref,
    behind_ref,
    ahead_ref,
    lower_z_ref,
    lower_x_ref,
    *refs,
):
    refs = list(refs)
    sems = refs.pop()
    hot_ref, values_ref, turned_ref = [refs.pop() for _ in range(3)]
    big = [refs.pop() for _ in range(6)]
    field_ref, source_ref, face_z_ref, face_x_ref, face_y_ref, diag_ref = big
    depth, width, lateral = field_ref.shape
    if first:
        link_ref = refs.pop()
    if not last:
        new_ref, out_ref = refs.pop(), refs.pop()
    linked_reads = begin([(turned_hbm, turned_ref)], sems)
    reads = begin(
        list(
            zip(
                (field_hbm, source_hbm, face_z_hbm, face_x_hbm, face_y_hbm, diag_hbm),
                big,
            )
        ),
        sems,
        2,
    )
    fill_hot(hot_ref, cell_ref[...])
    finish(linked_reads)
    for q in range(incoming_ref.shape[0]):
        turned = turned_ref[q]
        if first:
            turned = turned.T
            turned_ref[q] = turned
            put_halves(link_ref, q, turned)
        put_halves(values_ref, q, turned * incoming_ref[q].astype(F32))
    linked = scatter_lines(hot_ref, values_ref)
    if first:
        conduct = scatter_lines(hot_ref, link_ref)
        last_z = lax.axis_index("slab") == lax.axis_size("slab") - 1
        last_x = lax.axis_index("col") == lax.axis_size("col") - 1
    finish(reads)
    writes = []
    if last:
        fault_ref, own_ref, new_ref, fault_hot_ref, press_ref = refs
    elif first:
        new_hbm, out_hbm, turned_out, inverse_out = refs[:4]
        up_ref, down_ref, right_ref, left_ref = refs[4:]
        writes += begin([(turned_ref, turned_out)], sems, 8)
    else:
        new_hbm, out_hbm, up_ref, down_ref, right_ref, left_ref = refs
    across = iota((width, lateral), 0)
    along = iota((width, lateral), 1)
    for i in range(depth):
        field = field_ref[i]
        face_z = face_z_ref[i]
        lower_z = face_z_ref[i - 1] if i > 0 else lower_z_ref[1]
        above = field_ref[i + 1] if i < depth - 1 else above_ref[...]
        below = field_ref[i - 1] if i > 0 else below_ref[0]
        total = source_ref[i] + linked[i * width : (i + 1) * width]
        total = total + face_z * above + lower_z * below
        face_x = face_x_ref[i]
        lower_x = lower_x_ref[1, i : i + 1, :]
        ahead = jnp.where(
            across == width - 1, ahead_ref[i : i + 1, :], pltpu.roll(field, width - 1, 0)
        )
        flow = jnp.where(
            across == 0,
            lower_x * behind_ref[0, i : i + 1, :],
            pltpu.roll(face_x * field, 1, 0),
        )
        total = total + face_x * ahead + flow
        face_y = jnp.where(along == lateral - 1, 0.0, face_y_ref[i])
        total = total + face_y * pltpu.roll(field, lateral - 1, 1)
        total = total + pltpu.roll(face_y * field, 1, 1)
        if first:
            whole = diag_ref[i] + conduct[i * width : (i + 1) * width] + lower_z
            own_z = jnp.where(last_z, 0.0, face_z) if i == depth - 1 else face_z
            whole = whole + own_z + face_y + pltpu.roll(face_y, 1, 1)
            whole = whole + jnp.where((across == width - 1) & last_x, 0.0, face_x)
            whole = whole + jnp.where(across == 0, lower_x, pltpu.roll(face_x, 1, 0))
            inverse = 1.0 / whole
            diag_ref[i] = inverse
        else:
            inverse = diag_ref[i]
        new_ref[i] = total * inverse
    lines = new_ref[...].reshape(depth * width, lateral)
    if last:
        fill_hot(fault_hot_ref, fault_ref[...] >> 7)
        high, low = halves(lines.T)
        both = jnp.concatenate([high, low], 0)
        side = iota((lateral, 128), 0)
        for q in range(fault_ref.shape[0]):
            got = jnp.dot(
                both, fault_hot_ref[:, q * 128 : (q + 1) * 128], preferred_element_type=F32
            )
            got = got[:lateral] + got[lateral:]
            lane = fault_ref[q : q + 1, :] & 127
            got = jnp.sum(jnp.where(side == lane, got, 0.0), 0, keepdims=True)
            press_ref[0, q : q + 1, :] = got
        press_ref[0, fault_ref.shape[0] :, :] = own_ref[...]
        mine = press_ref[0]
        for o in range(1, press_ref.shape[0]):
            press_ref[o] = mine
    else:
        writes += begin([(new_ref, new_hbm)], sems, 9)
        if first:
            writes += begin([(diag_ref, inverse_out)], sems, 10)
        gather_lines(hot_ref, lines, out_ref)
        writes += begin([(out_ref, out_hbm)], sems, 11)
        up_ref[0] = new_ref[depth - 1]
        down_ref[...] = new_ref[0]
        for i in range(depth):
            right_ref[0, i : i + 1, :] = new_ref[i, width - 1 : width, :]
            left_ref[i : i + 1, :] = new_ref[i, 0:1, :]
    finish(writes)


def couple(cols_ref, tiles_ref, blocks_ref):
    rows, per = blocks_ref.shape[:2]
    ids = iota((rows, 128), 0)
    total = None
    for r in range(rows):
        for b in range(per):
            at = pl.ds(cols_ref[r, b], 1)
            left = [
                jnp.where(ids == r, tiles_ref[p, at, :], 0.0)
                for p in range(tiles_ref.shape[0])
            ]
            left = jnp.concatenate(left, 0).astype(BF16)
            part = lax.dot_general(left, blocks_ref[r, b], NT, preferred_element_type=F32)
            total = part if total is None else total + part
    return total


def contact_kernel(
    cols_ref,
    whole_ref,
    blocks_hbm,
    base_ref,
    slip_ref,
    stiff_ref,
    active_ref,
    own_ref,
    tiles_ref,
    blocks_ref,
    sems,
):
    reads = begin([(blocks_hbm, blocks_ref)], sems)
    owners = whole_ref.shape[0]
    rows = base_ref.shape[1]
    for p in range(3):
        part = whole_ref[:, p * rows : (p + 1) * rows, :].astype(F32)
        tiles_ref[p] = part.reshape(owners * rows, 128)
    finish(reads)
    coupled = couple(cols_ref, tiles_ref, blocks_ref)
    gain = active_ref[0].astype(F32) / stiff_ref[...]
    parts = [
        slip_ref[p] + gain * (base_ref[p] - coupled[p * rows : (p + 1) * rows])
        for p in range(3)
    ]
    own_ref[...] = jnp.concatenate([parts[0], -BIOT * gain, parts[1], parts[2]], 0)


def tail_kernel(
    cols_ref,
    whole_ref,
    blocks_ref,
    base_ref,
    own_ref,
    stiff_ref,
    active_ref,
    normal_ref,
    slip_ref,
    traction_ref,
    press_ref,
    tiles_ref,
):
    sources = whole_ref.shape[0]
    rows = base_ref.shape[1]
    ids = sources * rows
    for c in range(sources):
        for o in range(sources):
            n = o * rows + c
            press_ref[n : n + 1, :] = whole_ref[c, o : o + 1, :]

    def part(n):
        return whole_ref[:, (n + 1) * rows : (n + 2) * rows, :].reshape(ids, 128)

    slips = [part(0) + part(1) * press_ref[...], part(2), part(3)]
    for p in range(3):
        tiles_ref[p] = slips[p].astype(BF16).astype(F32)
    coupled = couple(cols_ref, tiles_ref, blocks_ref)
    mine = press_ref[pl.ds(pl.multiple_of(lax.axis_index("col") * rows, rows), rows), :]
    gain = active_ref[1].astype(F32) / stiff_ref[...]
    own = [own_ref[n * rows : (n + 1) * rows] for n in range(4)]
    slips = [own[0] + own[1] * mine, own[2], own[3]]
    loads = [base_ref[0] - BIOT * mine, base_ref[1], base_ref[2]]
    for p in range(3):
        traction = loads[p] - coupled[p * rows : (p + 1) * rows]
        traction_ref[p] = traction
        slip_ref[p] = slips[p] + gain * traction
        if p == 0:
            normal_ref[...] = traction


def back_kernel(
    normal_ref, fault_ref, fault_hot_ref, field_ref, inverse_ref, out_ref, values_ref
):
    depth, width, lateral = field_ref.shape
    side = iota((lateral, 128), 0)
    for q in range(normal_ref.shape[0]):
        lane = fault_ref[q : q + 1, :] & 127
        put_halves(values_ref, q, jnp.where(side == lane, normal_ref[q : q + 1, :], 0.0))
    returned = scatter_lines(fault_hot_ref, values_ref).reshape(depth, width, lateral)
    out_ref[...] = field_ref[...] + returned * inverse_ref[...]


def shift(block, axis, step):
    count = lax.axis_size(axis)
    route = [(i, i + step) for i in range(count) if 0 <= i + step < count]
    return lax.ppermute(block, axis, route)


def swap(blocks, axis):
    return lax.all_to_all(blocks, axis, split_axis=0, concat_axis=0, tiled=True)


def per_device(
    pressure,
    source,
    accum,
    trans_z,
    trans_x,
    trans_y,
    nnc_cell,
    nnc_trans,
    fault_cell,
    base_stress,
    slip_start,
    stiff_diag,
    active_set,
    mortar_blocks,
    mortar_cols,
):
    depth, width, lateral = pressure.shape
    slabs = lax.axis_size("slab")
    columns = lax.axis_size("col")
    lines = depth * width
    grid = ((depth, width, lateral), F32)
    slots = slabs * 128
    nodes = columns * 128
    rows = mortar_blocks.shape[1]
    cells = nnc_cell[0, 0]
    faults = fault_cell[0, 0]
    blocks = mortar_blocks[0]
    tile_cols = mortar_cols[0]
    base = base_stress[0].reshape(3, rows, 128)
    slip0 = slip_start[0].reshape(3, rows, 128)
    stiff = stiff_diag[0].reshape(rows, 128)
    active = active_set[:, 0].reshape(-1, rows, 128)
    tiles = pltpu.VMEM((3, columns * rows, 128), F32)
    layer, wall = (width, lateral), (depth, lateral)
    table = pltpu.VMEM((lines, slots), BF16)
    block = pltpu.VMEM((depth, width, lateral), F32)
    packet = pltpu.VMEM((slabs, lateral, 128), BF16)
    values = pltpu.VMEM((2 * lateral, slots), BF16)
    edges = [((1, *layer), F32), (layer, F32), ((1, *wall), F32), (wall, F32)]

    (ready,) = call(ready_kernel, [((columns, 3 * rows, 128), BF16)], slip0)
    whole = swap(ready, "col")
    outgoing, up, down, right, left = call(
        first_kernel,
        [
            ((slabs, lateral, 128), BF16, 0),
            ((2, *layer), F32),
            (layer, F32),
            ((2, *wall), F32),
            (wall, F32),
        ],
        pressure,
        trans_z,
        trans_x,
        cells,
        hbm=(0, 1, 2),
        scratch=(
            table,
            block,
            pltpu.VMEM((depth, 8, lateral), F32),
            packet,
            pltpu.SemaphoreType.DMA((4,)),
        ),
    )
    whole, outgoing = lax.optimization_barrier((whole, outgoing))
    incoming = swap(outgoing, "slab")
    below = lower_z = shift(up, "slab", 1)
    behind = lower_x = shift(right, "col", 1)
    above = shift(down, "slab", -1)
    ahead = shift(left, "col", -1)
    turned, diag = nnc_trans[0, 0], accum
    field = pressure
    for sweep in range(ITERS_FLOW):
        first = sweep == 0
        last = sweep == ITERS_FLOW - 1
        extra = [faults, own] if last else []
        if last:
            outs = [
                (grid[0], F32),
                ((lines, nodes), BF16),
                ((columns, columns + 4 * rows, 128), F32),
            ]
        else:
            outs = [(*grid, 0), ((slabs, lateral, 128), BF16, 0)]
            if first:
                outs += [((slabs, lateral, 128), F32, 0), (*grid, 0)]
            outs += edges
        got = call(
            functools.partial(sweep_kernel, first, last),
            outs,
            incoming,
            turned,
            field,
            source,
            trans_z,
            trans_x,
            trans_y,
            diag,
            cells,
            below,
            above,
            behind,
            ahead,
            lower_z,
            lower_x,
            *extra,
            hbm=range(1, 8),
            scratch=[
                *([] if last else [packet, block]),
                *([values] if first else []),
                *[block] * 6,
                pltpu.VMEM((slabs, lateral, 128), F32),
                values,
                table,
                pltpu.SemaphoreType.DMA((12,)),
            ],
        )
        if last:
            field, fault_hot, whole = got
            break
        if first:
            turned, diag = got[2:4]
            whole, _ = lax.optimization_barrier((whole, got[-1]))
        field, outgoing = got[:2]
        up, down, right, left = got[-4:]
        incoming = swap(outgoing, "slab")
        below = shift(up, "slab", 1)
        behind = shift(right, "col", 1)
        above = shift(down, "slab", -1)
        ahead = shift(left, "col", -1)
        if first:
            (own,) = call(
                contact_kernel,
                [((4 * rows, 128), F32)],
                tile_cols,
                whole,
                blocks,
                base,
                slip0,
                stiff,
                active,
                smem=(0,),
                hbm=(2,),
                scratch=(
                    tiles,
                    pltpu.VMEM(blocks.shape, BF16),
                    pltpu.SemaphoreType.DMA((1,)),
                ),
            )
    whole = swap(whole, "col")
    normal, slip, traction = call(
        tail_kernel,
        [((rows, 128), F32), ((3, rows, 128), F32), ((3, rows, 128), F32)],
        tile_cols,
        whole,
        blocks,
        base,
        own,
        stiff,
        active,
        smem=(0,),
        scratch=(pltpu.VMEM((columns * rows, 128), F32), tiles),
    )
    normal = swap(normal.reshape(columns, -1, 128), "col").reshape(columns, 128)
    (pressure_out,) = call(
        back_kernel,
        [grid],
        normal,
        faults,
        fault_hot,
        field,
        diag,
        scratch=(pltpu.VMEM((2 * lateral, nodes), BF16),),
    )
    return (pressure_out, slip.reshape(1, 3, -1), traction.reshape(1, 3, -1))


def solution(mesh):
    return jax.shard_map(
        per_device,
        mesh=mesh,
        in_specs=(
            P("slab", "col", None),
            P("slab", "col", None),
            P("slab", "col", None),
            P("slab", "col", None),
            P("slab", "col", None),
            P("slab", "col", None),
            P("slab", "col", None, None),
            P("slab", "col", None, None, None),
            P("slab", "col", None, None),
            P("slab", None, "col"),
            P("slab", None, "col"),
            P("slab", "col"),
            P(None, "slab", "col"),
            P("slab", "col", None, None, None),
            P("slab", "col", None),
        ),
        out_specs=(P("slab", "col", None), P("slab", None, "col"), P("slab", None, "col")),
        check_vma=False,
    )
```

```python
import functools

import jax
import jax.numpy as jnp
from jax import lax
from jax.experimental import pallas as pl
from jax.experimental.pallas import tpu as pltpu
from jax.sharding import PartitionSpec as P

ITERS_FLOW = 3
BIOT = 0.8
F32 = jnp.float32
BF16 = jnp.bfloat16
NT = (((1,), (1,)), ((), ()))


def call(body, outs, *args, smem=(), hbm=(), scratch=(), mib=14):
    spaces = [
        pltpu.SMEM if i in smem else pltpu.HBM if i in hbm else pltpu.VMEM
        for i in range(len(args))
    ]
    args = [
        pltpu.with_memory_space_constraint(a, pltpu.HBM) if i in hbm else a
        for i, a in enumerate(args)
    ]
    far = [len(o) > 2 for o in outs]
    return pl.pallas_call(
        body,
        in_specs=[pl.BlockSpec(memory_space=space) for space in spaces],
        out_specs=[
            pl.BlockSpec(memory_space=pltpu.HBM if f else pltpu.VMEM) for f in far
        ],
        out_shape=[
            pltpu.HBM(*o[:2]) if f else jax.ShapeDtypeStruct(*o)
            for o, f in zip(outs, far)
        ],
        scratch_shapes=list(scratch),
        compiler_params=pltpu.CompilerParams(vmem_limit_bytes=mib << 20),
    )(*args)


def begin(pairs, sems, at=0):
    copies = [
        pltpu.make_async_copy(source, target, sems.at[at + i])
        for i, (source, target) in enumerate(pairs)
    ]
    for copy in copies:
        copy.start()
    return copies


def finish(copies):
    for copy in copies:
        copy.wait()


def iota(shape, dim):
    return lax.broadcasted_iota(jnp.int32, shape, dim)


def halves(x):
    high = x.astype(BF16)
    return high, (x - high.astype(F32)).astype(BF16)


def fill_hot(hot_ref, lines):
    rows = hot_ref.shape[0]
    ids = iota((rows, 128), 0)
    for q in range(lines.shape[0]):
        hit = ids == lines[q : q + 1, :]
        hot_ref[:, q * 128 : (q + 1) * 128] = jnp.where(hit, 1.0, 0.0).astype(BF16)


def gather_lines(hot_ref, field, out_ref):
    turned = field.T.astype(BF16)
    for q in range(0, out_ref.shape[0], 2):
        got = jnp.dot(
            turned, hot_ref[:, q * 128 : (q + 2) * 128], preferred_element_type=F32
        ).astype(BF16)
        out_ref[q] = got[:, :128]
        out_ref[q + 1] = got[:, 128:]


def scatter_lines(hot_ref, values_ref):
    both = lax.dot_general(hot_ref[...], values_ref[...], NT, preferred_element_type=F32)
    return both[:, :128] + both[:, 128:]


def put_halves(values_ref, q, values):
    high, low = halves(values)
    values_ref[:128, q * 128 : (q + 1) * 128] = high
    values_ref[128:, q * 128 : (q + 1) * 128] = low


def odd(axis):
    return lax.axis_index(axis) % 2 == 1


def put_edges(field_ref, edge_refs):
    z_one, z_two, x_one, x_two = edge_refs
    depth, width, _ = field_ref.shape
    swap_z, swap_x = odd("slab"), odd("col")
    head, tail = field_ref[0], field_ref[depth - 1]
    z_one[0] = jnp.where(swap_z, head, tail)
    z_two[0] = jnp.where(swap_z, tail, head)
    for i in range(depth):
        head, tail = field_ref[i, 0:1, :], field_ref[i, width - 1 : width, :]
        x_one[0, i : i + 1, :] = jnp.where(swap_x, head, tail)
        x_two[0, i : i + 1, :] = jnp.where(swap_x, tail, head)


def first_kernel(
    field_hbm,
    face_z_hbm,
    face_x_hbm,
    slip_hbm,
    cell_ref,
    out_hbm,
    ready_hbm,
    kept_ref,
    z_one,
    z_two,
    x_one,
    x_two,
    hot_ref,
    field_ref,
    wall_ref,
    slip_ref,
    out_ref,
    ready_ref,
    sems,
):
    depth, width, lateral = field_ref.shape
    reads = begin(
        [
            (field_hbm, field_ref),
            (face_x_hbm.at[:, pl.ds(width - 8, 8), :], wall_ref),
            (face_z_hbm.at[depth - 1], z_one.at[1]),
            (face_z_hbm.at[depth - 1], z_two.at[1]),
            (slip_hbm, slip_ref),
        ],
        sems,
    )
    kept_ref[...] = cell_ref[...]
    fill_hot(hot_ref, cell_ref[...])
    finish(reads)
    gather_lines(hot_ref, field_ref[...].reshape(depth * width, lateral), out_ref)
    writes = begin([(out_ref, out_hbm)], sems, 5)
    parts, rows, _ = slip_ref.shape
    for p in range(parts):
        ready_ref[0, p * rows : (p + 1) * rows, :] = slip_ref[p].astype(BF16)
    mine = ready_ref[0]
    for o in range(1, ready_ref.shape[0]):
        ready_ref[o] = mine
    writes += begin([(ready_ref, ready_hbm)], sems, 6)
    put_edges(field_ref, (z_one, z_two, x_one, x_two))
    for i in range(depth):
        x_one[1, i : i + 1, :] = wall_ref[i, 7:8, :]
        x_two[1, i : i + 1, :] = wall_ref[i, 7:8, :]
    finish(writes)


def sweep_kernel(
    first,
    last,
    incoming_ref,
    turned_hbm,
    field_hbm,
    source_hbm,
    face_z_hbm,
    face_x_hbm,
    face_y_hbm,
    diag_hbm,
    cell_ref,
    z_one,
    z_two,
    x_one,
    x_two,
    *refs,
):
    refs = list(refs)
    sems = refs.pop()
    hot_ref, values_ref, turned_ref = [refs.pop() for _ in range(3)]
    big = [refs.pop() for _ in range(6)]
    field_ref, source_ref, face_z_ref, face_x_ref, face_y_ref, diag_ref = big
    depth, width, lateral = field_ref.shape
    if first:
        link_ref = refs.pop()
    if not last:
        new_ref, out_ref = refs.pop(), refs.pop()
    faces = [z_one, z_two, x_one, x_two] if first else [refs.pop(0) for _ in range(4)]
    linked_reads = begin([(turned_hbm, turned_ref)], sems)
    reads = begin(
        list(
            zip(
                (field_hbm, source_hbm, face_z_hbm, face_x_hbm, face_y_hbm, diag_hbm),
                big,
            )
        ),
        sems,
        2,
    )
    fill_hot(hot_ref, cell_ref[...])
    finish(linked_reads)
    for q in range(incoming_ref.shape[0]):
        turned = turned_ref[q]
        if first:
            turned = turned.T
            turned_ref[q] = turned
            put_halves(link_ref, q, turned)
        put_halves(values_ref, q, turned * incoming_ref[q].astype(F32))
    linked = scatter_lines(hot_ref, values_ref)
    if first:
        conduct = scatter_lines(hot_ref, link_ref)
        last_z = lax.axis_index("slab") == lax.axis_size("slab") - 1
        last_x = lax.axis_index("col") == lax.axis_size("col") - 1
    finish(reads)
    writes = []
    if last:
        fault_ref, own_ref, new_ref, fault_hot_ref, press_ref = refs
    elif first:
        new_hbm, out_hbm, turned_out, inverse_out = refs[:4]
        edge_refs = refs[4:]
        writes += begin([(turned_ref, turned_out)], sems, 8)
    else:
        new_hbm, out_hbm = refs[:2]
        edge_refs = refs[2:]
    swap_z, swap_x = odd("slab"), odd("col")
    below_z = jnp.where(swap_z, z_one[0], z_two[0])
    above_z = jnp.where(swap_z, z_two[0], z_one[0])
    edge_z = jnp.where(swap_z, faces[0][1], faces[1][1])
    behind_x = jnp.where(swap_x, x_one[0], x_two[0])
    ahead_x = jnp.where(swap_x, x_two[0], x_one[0])
    edge_x = jnp.where(swap_x, faces[2][1], faces[3][1])
    across = iota((width, lateral), 0)
    along = iota((width, lateral), 1)
    for i in range(depth):
        field = field_ref[i]
        face_z = face_z_ref[i]
        lower_z = face_z_ref[i - 1] if i > 0 else edge_z
        above = field_ref[i + 1] if i < depth - 1 else above_z
        below = field_ref[i - 1] if i > 0 else below_z
        total = source_ref[i] + linked[i * width : (i + 1) * width]
        total = total + face_z * above + lower_z * below
        face_x = face_x_ref[i]
        lower_x = edge_x[i : i + 1, :]
        ahead = jnp.where(
            across == width - 1, ahead_x[i : i + 1, :], pltpu.roll(field, width - 1, 0)
        )
        flow = jnp.where(
            across == 0,
            lower_x * behind_x[i : i + 1, :],
            pltpu.roll(face_x * field, 1, 0),
        )
        total = total + face_x * ahead + flow
        face_y = jnp.where(along == lateral - 1, 0.0, face_y_ref[i])
        total = total + face_y * pltpu.roll(field, lateral - 1, 1)
        total = total + pltpu.roll(face_y * field, 1, 1)
        if first:
            whole = diag_ref[i] + conduct[i * width : (i + 1) * width] + lower_z
            own_z = jnp.where(last_z, 0.0, face_z) if i == depth - 1 else face_z
            whole = whole + own_z + face_y + pltpu.roll(face_y, 1, 1)
            whole = whole + jnp.where((across == width - 1) & last_x, 0.0, face_x)
            whole = whole + jnp.where(across == 0, lower_x, pltpu.roll(face_x, 1, 0))
            inverse = 1.0 / whole
            diag_ref[i] = inverse
        else:
            inverse = diag_ref[i]
        new_ref[i] = total * inverse
    lines = new_ref[...].reshape(depth * width, lateral)
    if last:
        fill_hot(fault_hot_ref, fault_ref[...] >> 7)
        high, low = halves(lines.T)
        both = jnp.concatenate([high, low], 0)
        side = iota((lateral, 128), 0)
        for q in range(fault_ref.shape[0]):
            got = jnp.dot(
                both, fault_hot_ref[:, q * 128 : (q + 1) * 128], preferred_element_type=F32
            )
            got = got[:lateral] + got[lateral:]
            lane = fault_ref[q : q + 1, :] & 127
            got = jnp.sum(jnp.where(side == lane, got, 0.0), 0, keepdims=True)
            face_x_ref[0, q : q + 1, :] = got
        rows = fault_ref.shape[0]
        planes = [
            *halves(face_x_ref[0, :rows, :]),
            *halves(own_ref[:rows]),
            *[own_ref[n * rows : (n + 1) * rows].astype(BF16) for n in (1, 2, 3)],
        ]
        for n, plane in enumerate(planes):
            press_ref[0, n * rows : (n + 1) * rows, :] = plane
        mine = press_ref[0]
        for o in range(1, press_ref.shape[0]):
            press_ref[o] = mine
    else:
        writes += begin([(new_ref, new_hbm)], sems, 9)
        if first:
            writes += begin([(diag_ref, inverse_out)], sems, 10)
        gather_lines(hot_ref, lines, out_ref)
        writes += begin([(out_ref, out_hbm)], sems, 11)
        put_edges(new_ref, edge_refs)
    finish(writes)


def couple(cols_ref, tiles_ref, blocks_ref):
    rows, per = blocks_ref.shape[:2]
    ids = iota((rows, 128), 0)
    total = None
    for r in range(rows):
        for b in range(per):
            at = pl.ds(cols_ref[r, b], 1)
            left = [
                jnp.where(ids == r, tiles_ref[p, at, :], 0.0)
                for p in range(tiles_ref.shape[0])
            ]
            left = jnp.concatenate(left, 0).astype(BF16)
            part = lax.dot_general(left, blocks_ref[r, b], NT, preferred_element_type=F32)
            total = part if total is None else total + part
    return total


def contact_kernel(
    cols_ref,
    whole_ref,
    blocks_hbm,
    base_ref,
    slip_ref,
    stiff_ref,
    active_ref,
    own_ref,
    tiles_ref,
    blocks_ref,
    sems,
):
    reads = begin([(blocks_hbm, blocks_ref)], sems)
    owners = whole_ref.shape[0]
    rows = base_ref.shape[1]
    for p in range(3):
        part = whole_ref[:, p * rows : (p + 1) * rows, :].astype(F32)
        tiles_ref[p] = part.reshape(owners * rows, 128)
    finish(reads)
    coupled = couple(cols_ref, tiles_ref, blocks_ref)
    gain = active_ref[0].astype(F32) / stiff_ref[...]
    parts = [
        slip_ref[p] + gain * (base_ref[p] - coupled[p * rows : (p + 1) * rows])
        for p in range(3)
    ]
    own_ref[...] = jnp.concatenate([parts[0], -BIOT * gain, parts[1], parts[2]], 0)


def tail_kernel(
    cols_ref,
    whole_ref,
    blocks_ref,
    base_ref,
    own_ref,
    stiff_ref,
    active_ref,
    normal_ref,
    slip_ref,
    traction_ref,
    press_ref,
    tiles_ref,
):
    sources = whole_ref.shape[0]
    rows = base_ref.shape[1]
    ids = sources * rows
    def part(n):
        plane = whole_ref[:, n * rows : (n + 1) * rows, :].astype(F32)
        return plane.reshape(ids, 128)

    for c in range(sources):
        press = whole_ref[c, :rows, :].astype(F32) + whole_ref[c, rows : 2 * rows, :]
        press_ref[pl.ds(c, sources, stride=rows), :] = press
    slips = [part(2) + part(3) + part(4) * press_ref[...], part(5), part(6)]
    for p in range(3):
        tiles_ref[p] = slips[p].astype(BF16).astype(F32)
    coupled = couple(cols_ref, tiles_ref, blocks_ref)
    mine = press_ref[pl.ds(pl.multiple_of(lax.axis_index("col") * rows, rows), rows), :]
    gain = active_ref[1].astype(F32) / stiff_ref[...]
    own = [own_ref[n * rows : (n + 1) * rows] for n in range(4)]
    slips = [own[0] + own[1] * mine, own[2], own[3]]
    loads = [base_ref[0] - BIOT * mine, base_ref[1], base_ref[2]]
    for p in range(3):
        traction = loads[p] - coupled[p * rows : (p + 1) * rows]
        traction_ref[p] = traction
        slip_ref[p] = slips[p] + gain * traction
        if p == 0:
            normal_ref[...] = traction


def back_kernel(
    normal_ref, fault_ref, fault_hot_ref, field_ref, inverse_ref, out_ref, values_ref
):
    depth, width, lateral = field_ref.shape
    side = iota((lateral, 128), 0)
    for q in range(normal_ref.shape[0]):
        lane = fault_ref[q : q + 1, :] & 127
        put_halves(values_ref, q, jnp.where(side == lane, normal_ref[q : q + 1, :], 0.0))
    returned = scatter_lines(fault_hot_ref, values_ref).reshape(depth, width, lateral)
    out_ref[...] = field_ref[...] + returned * inverse_ref[...]


def exchange(edges):
    got = []
    for edge, (axis, start) in zip(edges, (("slab", 0), ("slab", 1), ("col", 0), ("col", 1))):
        count = lax.axis_size(axis)
        pairs = [(i, i + 1) for i in range(start, count - 1, 2)]
        got.append(lax.ppermute(edge, axis, pairs + [(j, i) for i, j in pairs]))
    return got


def swap(blocks, axis):
    return lax.all_to_all(blocks, axis, split_axis=0, concat_axis=0, tiled=True)


def per_device(
    pressure,
    source,
    accum,
    trans_z,
    trans_x,
    trans_y,
    nnc_cell,
    nnc_trans,
    fault_cell,
    base_stress,
    slip_start,
    stiff_diag,
    active_set,
    mortar_blocks,
    mortar_cols,
):
    depth, width, lateral = pressure.shape
    slabs = lax.axis_size("slab")
    columns = lax.axis_size("col")
    lines = depth * width
    grid = ((depth, width, lateral), F32)
    slots = slabs * 128
    nodes = columns * 128
    rows = mortar_blocks.shape[1]
    cells = nnc_cell[0, 0]
    faults = fault_cell[0, 0]
    blocks = mortar_blocks[0]
    tile_cols = mortar_cols[0]
    base = base_stress[0].reshape(3, rows, 128)
    slip0 = slip_start[0].reshape(3, rows, 128)
    stiff = stiff_diag[0].reshape(rows, 128)
    active = active_set[:, 0].reshape(-1, rows, 128)
    tiles = pltpu.VMEM((3, columns * rows, 128), F32)
    layer, wall = (width, lateral), (depth, lateral)
    table = pltpu.VMEM((lines, slots), BF16)
    block = pltpu.VMEM((depth, width, lateral), F32)
    packet = pltpu.VMEM((slabs, lateral, 128), BF16)
    values = pltpu.VMEM((2 * lateral, slots), BF16)
    edges = [((1, *layer), F32)] * 2 + [((1, *wall), F32)] * 2
    doubled = [((2, *layer), F32)] * 2 + [((2, *wall), F32)] * 2
    planes = 7 * rows

    outgoing, ready, cells, *sides = call(
        first_kernel,
        [
            ((slabs, lateral, 128), BF16, 0),
            ((columns, 3 * rows, 128), BF16, 0),
            (cells.shape, jnp.int32),
            *doubled,
        ],
        pressure,
        trans_z,
        trans_x,
        slip0,
        cells,
        hbm=(0, 1, 2, 3),
        scratch=(
            table,
            block,
            pltpu.VMEM((depth, 8, lateral), F32),
            pltpu.VMEM(slip0.shape, F32),
            packet,
            pltpu.VMEM((columns, 3 * rows, 128), BF16),
            pltpu.SemaphoreType.DMA((7,)),
        ),
    )
    incoming = swap(outgoing, "slab")
    sides = exchange(sides)
    ready, incoming, sides = lax.optimization_barrier((ready, incoming, sides))
    faces = sides
    whole = swap(ready, "col")
    turned, diag = nnc_trans[0, 0], accum
    field = pressure
    for sweep in range(ITERS_FLOW):
        first = sweep == 0
        last = sweep == ITERS_FLOW - 1
        extra = [] if first else list(faces)
        if last:
            extra += [faults, own]
            outs = [
                (grid[0], F32),
                ((lines, nodes), BF16),
                ((columns, planes, 128), BF16),
            ]
        else:
            outs = [(*grid, 0), ((slabs, lateral, 128), BF16, 0)]
            if first:
                outs += [((slabs, lateral, 128), F32, 0), (*grid, 0)]
            outs += edges
        got = call(
            functools.partial(sweep_kernel, first, last),
            outs,
            incoming,
            turned,
            field,
            source,
            trans_z,
            trans_x,
            trans_y,
            diag,
            cells,
            *sides,
            *extra,
            hbm=range(1, 8),
            scratch=[
                *([] if last else [packet, block]),
                *([values] if first else []),
                *[block] * 6,
                pltpu.VMEM((slabs, lateral, 128), F32),
                values,
                table,
                pltpu.SemaphoreType.DMA((12,)),
            ],
        )
        if last:
            field, fault_hot, whole = got
            break
        field, outgoing = got[:2]
        if first:
            turned, diag = got[2:4]
            whole, outgoing = lax.optimization_barrier((whole, outgoing))
        incoming = swap(outgoing, "slab")
        sides = exchange(got[-4:])
        if first:
            (own,) = call(
                contact_kernel,
                [((4 * rows, 128), F32)],
                tile_cols,
                whole,
                blocks,
                base,
                slip0,
                stiff,
                active,
                smem=(0,),
                hbm=(2,),
                scratch=(
                    tiles,
                    pltpu.VMEM(blocks.shape, BF16),
                    pltpu.SemaphoreType.DMA((1,)),
                ),
            )
    whole = swap(whole, "col")
    normal, slip, traction = call(
        tail_kernel,
        [((rows, 128), F32), ((3, rows, 128), F32), ((3, rows, 128), F32)],
        tile_cols,
        whole,
        blocks,
        base,
        own,
        stiff,
        active,
        smem=(0,),
        scratch=(pltpu.VMEM((columns * rows, 128), F32), tiles),
    )
    normal = swap(normal.reshape(columns, -1, 128), "col").reshape(columns, 128)
    (pressure_out,) = call(
        back_kernel,
        [grid],
        normal,
        faults,
        fault_hot,
        field,
        diag,
        scratch=(pltpu.VMEM((2 * lateral, nodes), BF16),),
    )
    return (pressure_out, slip.reshape(1, 3, -1), traction.reshape(1, 3, -1))


def solution(mesh):
    return jax.shard_map(
        per_device,
        mesh=mesh,
        in_specs=(
            P("slab", "col", None),
            P("slab", "col", None),
            P("slab", "col", None),
            P("slab", "col", None),
            P("slab", "col", None),
            P("slab", "col", None),
            P("slab", "col", None, None),
            P("slab", "col", None, None, None),
            P("slab", "col", None, None),
            P("slab", None, "col"),
            P("slab", None, "col"),
            P("slab", "col"),
            P(None, "slab", "col"),
            P("slab", "col", None, None, None),
            P("slab", "col", None),
        ),
        out_specs=(P("slab", "col", None), P("slab", None, "col"), P("slab", None, "col")),
        check_vma=False,
    )
```

```python
import functools

import jax
import jax.numpy as jnp
from jax import lax
from jax.experimental import pallas as pl
from jax.experimental.pallas import tpu as pltpu
from jax.sharding import PartitionSpec as P

ITERS_FLOW = 3
BIOT = 0.8
STEPS = (1, 4, 8, 2)
F32 = jnp.float32
BF16 = jnp.bfloat16
NT = (((1,), (1,)), ((), ()))


def call(body, outs, *args, smem=(), hbm=(), scratch=(), mib=14):
    spaces = [
        pltpu.SMEM if i in smem else pltpu.HBM if i in hbm else pltpu.VMEM
        for i in range(len(args))
    ]
    args = [
        pltpu.with_memory_space_constraint(a, pltpu.HBM) if i in hbm else a
        for i, a in enumerate(args)
    ]
    far = [len(o) > 2 for o in outs]
    return pl.pallas_call(
        body,
        in_specs=[pl.BlockSpec(memory_space=space) for space in spaces],
        out_specs=[
            pl.BlockSpec(memory_space=pltpu.HBM if f else pltpu.VMEM) for f in far
        ],
        out_shape=[
            pltpu.HBM(*o[:2]) if f else jax.ShapeDtypeStruct(*o)
            for o, f in zip(outs, far)
        ],
        scratch_shapes=list(scratch),
        compiler_params=pltpu.CompilerParams(vmem_limit_bytes=mib << 20),
    )(*args)


def begin(pairs, sems, at=0):
    copies = [
        pltpu.make_async_copy(source, target, sems.at[at + i])
        for i, (source, target) in enumerate(pairs)
    ]
    for copy in copies:
        copy.start()
    return copies


def finish(copies):
    for copy in copies:
        copy.wait()


def iota(shape, dim):
    return lax.broadcasted_iota(jnp.int32, shape, dim)


def halves(x):
    high = x.astype(BF16)
    return high, (x - high.astype(F32)).astype(BF16)


def fill_hot(hot_ref, lines):
    rows = hot_ref.shape[0]
    ids = iota((rows, 128), 0)
    for q in range(lines.shape[0]):
        hit = ids == lines[q : q + 1, :]
        hot_ref[:, q * 128 : (q + 1) * 128] = jnp.where(hit, 1.0, 0.0).astype(BF16)


def gather_lines(hot_ref, field, out_ref):
    turned = field.T.astype(BF16)
    for q in range(0, out_ref.shape[0], 2):
        got = jnp.dot(
            turned, hot_ref[:, q * 128 : (q + 2) * 128], preferred_element_type=F32
        ).astype(BF16)
        out_ref[q] = got[:, :128]
        out_ref[q + 1] = got[:, 128:]


def scatter_lines(hot_ref, values_ref):
    both = lax.dot_general(hot_ref[...], values_ref[...], NT, preferred_element_type=F32)
    return both[:, :128] + both[:, 128:]


def put_halves(values_ref, q, values):
    high, low = halves(values)
    values_ref[:128, q * 128 : (q + 1) * 128] = high
    values_ref[128:, q * 128 : (q + 1) * 128] = low


def odd(axis):
    return lax.axis_index(axis) % 2 == 1


def put_edges(field_ref, edge_refs):
    z_one, z_two, x_one, x_two = edge_refs
    depth, width, _ = field_ref.shape
    swap_z, swap_x = odd("slab"), odd("col")
    head, tail = field_ref[0], field_ref[depth - 1]
    z_one[0] = jnp.where(swap_z, head, tail).astype(BF16)
    z_two[0] = jnp.where(swap_z, tail, head).astype(BF16)
    heads = jnp.concatenate([field_ref[i, 0:1, :] for i in range(depth)], 0)
    tails = jnp.concatenate(
        [field_ref[i, width - 1 : width, :] for i in range(depth)], 0
    )
    x_one[0] = jnp.where(swap_x, heads, tails).astype(BF16)
    x_two[0] = jnp.where(swap_x, tails, heads).astype(BF16)


def first_kernel(
    field_hbm,
    face_z_hbm,
    face_x_hbm,
    slip_hbm,
    cell_ref,
    out_hbm,
    ready_ref,
    kept_ref,
    z_one,
    z_two,
    x_one,
    x_two,
    hot_ref,
    field_ref,
    wall_ref,
    layer_ref,
    slip_ref,
    out_ref,
    sems,
):
    depth, width, lateral = field_ref.shape
    reads = begin(
        [
            (field_hbm, field_ref),
            (face_x_hbm.at[:, pl.ds(width - 8, 8), :], wall_ref),
            (face_z_hbm.at[depth - 1], layer_ref),
            (slip_hbm, slip_ref),
        ],
        sems,
    )
    kept_ref[...] = cell_ref[...]
    fill_hot(hot_ref, cell_ref[...])
    finish(reads)
    gather_lines(hot_ref, field_ref[...].reshape(depth * width, lateral), out_ref)
    writes = begin([(out_ref, out_hbm)], sems, 4)
    parts, rows, _ = slip_ref.shape
    for p in range(parts):
        ready_ref[0, p * rows : (p + 1) * rows, :] = slip_ref[p].astype(BF16)
    put_edges(field_ref, (z_one, z_two, x_one, x_two))
    layer = layer_ref[...].astype(BF16)
    wall = jnp.concatenate([wall_ref[i, 7:8, :] for i in range(depth)], 0).astype(BF16)
    z_one[1] = layer
    z_two[1] = layer
    x_one[1] = wall
    x_two[1] = wall
    finish(writes)


def pick(choice, one, two):
    return jnp.where(choice, one.astype(F32), two.astype(F32))


def sweep_kernel(
    first,
    last,
    incoming_ref,
    turned_hbm,
    field_hbm,
    source_hbm,
    face_z_hbm,
    face_x_hbm,
    face_y_hbm,
    diag_hbm,
    cell_ref,
    z_one,
    z_two,
    x_one,
    x_two,
    *refs,
):
    refs = list(refs)
    sems = refs.pop()
    hot_ref, values_ref, turned_ref = [refs.pop() for _ in range(3)]
    big = [refs.pop() for _ in range(6)]
    field_ref, source_ref, face_z_ref, face_x_ref, face_y_ref, diag_ref = big
    depth, width, lateral = field_ref.shape
    if first:
        link_ref = refs.pop()
    if not last:
        new_ref, out_ref = refs.pop(), refs.pop()
    faces = [z_one, z_two, x_one, x_two] if first else [refs.pop(0) for _ in range(4)]
    linked_reads = begin([(turned_hbm, turned_ref)], sems)
    reads = begin(
        list(
            zip(
                (field_hbm, source_hbm, face_z_hbm, face_x_hbm, face_y_hbm, diag_hbm),
                big,
            )
        ),
        sems,
        2,
    )
    if last:
        table_reads = begin([(refs[2], refs[4])], sems, 8)
    fill_hot(hot_ref, cell_ref[...])
    finish(linked_reads)
    for q in range(incoming_ref.shape[0]):
        turned = turned_ref[q]
        if first:
            turned = turned.T
            turned_ref[q] = turned
            put_halves(link_ref, q, turned)
        put_halves(values_ref, q, turned * incoming_ref[q].astype(F32))
    linked = scatter_lines(hot_ref, values_ref)
    if first:
        conduct = scatter_lines(hot_ref, link_ref)
        last_z = lax.axis_index("slab") == lax.axis_size("slab") - 1
        last_x = lax.axis_index("col") == lax.axis_size("col") - 1
    finish(reads)
    writes = []
    if last:
        fault_ref, own_ref, _, new_ref, fault_hot_ref, press_ref = refs
    elif first:
        new_hbm, out_hbm, turned_out, inverse_out = refs[:4]
        edge_refs = refs[4:]
        writes += begin([(turned_ref, turned_out)], sems, 8)
    else:
        new_hbm, out_hbm = refs[:2]
        edge_refs = refs[2:]
    swap_z, swap_x = odd("slab"), odd("col")
    below_z = pick(swap_z, z_one[0], z_two[0])
    above_z = pick(swap_z, z_two[0], z_one[0])
    edge_z = pick(swap_z, faces[0][1], faces[1][1])
    behind_x = pick(swap_x, x_one[0], x_two[0])
    ahead_x = pick(swap_x, x_two[0], x_one[0])
    edge_x = pick(swap_x, faces[2][1], faces[3][1])
    across = iota((width, lateral), 0)
    along = iota((width, lateral), 1)
    for i in range(depth):
        field = field_ref[i]
        face_z = face_z_ref[i]
        lower_z = face_z_ref[i - 1] if i > 0 else edge_z
        above = field_ref[i + 1] if i < depth - 1 else above_z
        below = field_ref[i - 1] if i > 0 else below_z
        total = source_ref[i] + linked[i * width : (i + 1) * width]
        total = total + face_z * above + lower_z * below
        face_x = face_x_ref[i]
        lower_x = edge_x[i : i + 1, :]
        ahead = jnp.where(
            across == width - 1, ahead_x[i : i + 1, :], pltpu.roll(field, width - 1, 0)
        )
        flow = jnp.where(
            across == 0,
            lower_x * behind_x[i : i + 1, :],
            pltpu.roll(face_x * field, 1, 0),
        )
        total = total + face_x * ahead + flow
        face_y = jnp.where(along == lateral - 1, 0.0, face_y_ref[i])
        total = total + face_y * pltpu.roll(field, lateral - 1, 1)
        total = total + pltpu.roll(face_y * field, 1, 1)
        if first:
            whole = diag_ref[i] + conduct[i * width : (i + 1) * width] + lower_z
            own_z = jnp.where(last_z, 0.0, face_z) if i == depth - 1 else face_z
            whole = whole + own_z + face_y + pltpu.roll(face_y, 1, 1)
            whole = whole + jnp.where((across == width - 1) & last_x, 0.0, face_x)
            whole = whole + jnp.where(across == 0, lower_x, pltpu.roll(face_x, 1, 0))
            inverse = 1.0 / whole
            diag_ref[i] = inverse
        else:
            inverse = diag_ref[i]
        new_ref[i] = total * inverse
    lines = new_ref[...].reshape(depth * width, lateral)
    if last:
        finish(table_reads)
        high, low = halves(lines.T)
        both = jnp.concatenate([high, low], 0)
        side = iota((lateral, 128), 0)
        for q in range(fault_ref.shape[0]):
            got = jnp.dot(
                both, fault_hot_ref[:, q * 128 : (q + 1) * 128], preferred_element_type=F32
            )
            got = got[:lateral] + got[lateral:]
            lane = fault_ref[q : q + 1, :] & 127
            got = jnp.sum(jnp.where(side == lane, got, 0.0), 0, keepdims=True)
            face_x_ref[0, q : q + 1, :] = got
        rows = fault_ref.shape[0]
        planes = [
            *halves(face_x_ref[0, :rows, :]),
            *halves(own_ref[:rows]),
            *[own_ref[n * rows : (n + 1) * rows].astype(BF16) for n in (1, 2, 3)],
        ]
        for n, plane in enumerate(planes):
            press_ref[0, n * rows : (n + 1) * rows, :] = plane
        mine = press_ref[0]
        for o in range(1, press_ref.shape[0]):
            press_ref[o] = mine
    else:
        writes += begin([(new_ref, new_hbm)], sems, 9)
        if first:
            writes += begin([(diag_ref, inverse_out)], sems, 10)
        gather_lines(hot_ref, lines, out_ref)
        writes += begin([(out_ref, out_hbm)], sems, 11)
        put_edges(new_ref, edge_refs)
    finish(writes)


def couple(cols_ref, tiles_ref, blocks_ref):
    rows, per = blocks_ref.shape[:2]
    ids = iota((rows, 128), 0)
    total = None
    for r in range(rows):
        for b in range(per):
            at = pl.ds(cols_ref[r, b], 1)
            left = [
                jnp.where(ids == r, tiles_ref[p, at, :], 0.0)
                for p in range(tiles_ref.shape[0])
            ]
            left = jnp.concatenate(left, 0).astype(BF16)
            part = lax.dot_general(left, blocks_ref[r, b], NT, preferred_element_type=F32)
            total = part if total is None else total + part
    return total


def contact_kernel(
    cols_ref,
    near_ref,
    far_ref,
    blocks_hbm,
    base_ref,
    slip_ref,
    stiff_ref,
    active_ref,
    fault_ref,
    own_ref,
    fault_hot_hbm,
    tiles_ref,
    blocks_ref,
    fault_hot_ref,
    sems,
):
    reads = begin([(blocks_hbm, blocks_ref)], sems)
    fill_hot(fault_hot_ref, fault_ref[...] >> 7)
    writes = begin([(fault_hot_ref, fault_hot_hbm)], sems, 1)
    rows = base_ref.shape[1]
    me = lax.axis_index("col")
    held = near_ref.shape[0]
    for n in range(2 * held):
        apart = sum(bit for k, bit in enumerate(STEPS) if n >> k & 1)
        owner = pl.multiple_of((me ^ apart) * rows, rows)
        for p in range(3):
            ref = near_ref if n < held else far_ref
            part = ref[n % held, p * rows : (p + 1) * rows, :].astype(F32)
            tiles_ref[p, pl.ds(owner, rows), :] = part
    finish(reads)
    coupled = couple(cols_ref, tiles_ref, blocks_ref)
    gain = active_ref[0].astype(F32) / stiff_ref[...]
    parts = [
        slip_ref[p] + gain * (base_ref[p] - coupled[p * rows : (p + 1) * rows])
        for p in range(3)
    ]
    own_ref[...] = jnp.concatenate([parts[0], -BIOT * gain, parts[1], parts[2]], 0)
    finish(writes)


def tail_kernel(
    cols_ref,
    whole_ref,
    blocks_ref,
    base_ref,
    own_ref,
    stiff_ref,
    active_ref,
    normal_ref,
    slip_ref,
    traction_ref,
    press_ref,
    tiles_ref,
):
    sources = whole_ref.shape[0]
    rows = base_ref.shape[1]
    ids = sources * rows
    def part(n):
        plane = whole_ref[:, n * rows : (n + 1) * rows, :].astype(F32)
        return plane.reshape(ids, 128)

    for c in range(sources):
        press = whole_ref[c, :rows, :].astype(F32) + whole_ref[c, rows : 2 * rows, :]
        press_ref[pl.ds(c, sources, stride=rows), :] = press
    slips = [part(2) + part(3) + part(4) * press_ref[...], part(5), part(6)]
    for p in range(3):
        tiles_ref[p] = slips[p].astype(BF16).astype(F32)
    coupled = couple(cols_ref, tiles_ref, blocks_ref)
    mine = press_ref[pl.ds(pl.multiple_of(lax.axis_index("col") * rows, rows), rows), :]
    gain = active_ref[1].astype(F32) / stiff_ref[...]
    own = [own_ref[n * rows : (n + 1) * rows] for n in range(4)]
    slips = [own[0] + own[1] * mine, own[2], own[3]]
    loads = [base_ref[0] - BIOT * mine, base_ref[1], base_ref[2]]
    for p in range(3):
        traction = loads[p] - coupled[p * rows : (p + 1) * rows]
        traction_ref[p] = traction
        slip_ref[p] = slips[p] + gain * traction
        if p == 0:
            normal_ref[...] = traction


def back_kernel(
    normal_ref, fault_ref, fault_hot_ref, field_ref, inverse_ref, out_ref, values_ref
):
    depth, width, lateral = field_ref.shape
    side = iota((lateral, 128), 0)
    for q in range(normal_ref.shape[0]):
        lane = fault_ref[q : q + 1, :] & 127
        put_halves(values_ref, q, jnp.where(side == lane, normal_ref[q : q + 1, :], 0.0))
    returned = scatter_lines(fault_hot_ref, values_ref).reshape(depth, width, lateral)
    out_ref[...] = field_ref[...] + returned * inverse_ref[...]


def exchange(edges):
    got = []
    for edge, (axis, start) in zip(edges, (("slab", 0), ("slab", 1), ("col", 0), ("col", 1))):
        count = lax.axis_size(axis)
        pairs = [(i, i + 1) for i in range(start, count - 1, 2)]
        got.append(lax.ppermute(edge, axis, pairs + [(j, i) for i, j in pairs]))
    return got


def paired(block, axis, apart):
    return lax.ppermute(block, axis, [(i, i ^ apart) for i in range(lax.axis_size(axis))])


def double(block, axis, apart):
    return jnp.concatenate([block, paired(block, axis, apart)], 0)


def swap(blocks, axis):
    return lax.all_to_all(blocks, axis, split_axis=0, concat_axis=0, tiled=True)


def per_device(
    pressure,
    source,
    accum,
    trans_z,
    trans_x,
    trans_y,
    nnc_cell,
    nnc_trans,
    fault_cell,
    base_stress,
    slip_start,
    stiff_diag,
    active_set,
    mortar_blocks,
    mortar_cols,
):
    depth, width, lateral = pressure.shape
    slabs = lax.axis_size("slab")
    columns = lax.axis_size("col")
    lines = depth * width
    grid = ((depth, width, lateral), F32)
    slots = slabs * 128
    nodes = columns * 128
    rows = mortar_blocks.shape[1]
    cells = nnc_cell[0, 0]
    faults = fault_cell[0, 0]
    blocks = mortar_blocks[0]
    tile_cols = mortar_cols[0]
    base = base_stress[0].reshape(3, rows, 128)
    slip0 = slip_start[0].reshape(3, rows, 128)
    stiff = stiff_diag[0].reshape(rows, 128)
    active = active_set[:, 0].reshape(-1, rows, 128)
    tiles = pltpu.VMEM((3, columns * rows, 128), F32)
    layer, wall = (width, lateral), (depth, lateral)
    table = pltpu.VMEM((lines, slots), BF16)
    block = pltpu.VMEM((depth, width, lateral), F32)
    packet = pltpu.VMEM((slabs, lateral, 128), BF16)
    values = pltpu.VMEM((2 * lateral, slots), BF16)
    edges = [((1, *layer), BF16)] * 2 + [((1, *wall), BF16)] * 2
    doubled = [((2, *layer), BF16)] * 2 + [((2, *wall), BF16)] * 2
    planes = 7 * rows

    outgoing, ready, cells, *sides = call(
        first_kernel,
        [
            ((slabs, lateral, 128), BF16, 0),
            ((1, 3 * rows, 128), BF16),
            (cells.shape, jnp.int32),
            *doubled,
        ],
        pressure,
        trans_z,
        trans_x,
        slip0,
        cells,
        hbm=(0, 1, 2, 3),
        scratch=(
            table,
            block,
            pltpu.VMEM((depth, 8, lateral), F32),
            pltpu.VMEM(layer, F32),
            pltpu.VMEM(slip0.shape, F32),
            packet,
            pltpu.SemaphoreType.DMA((5,)),
        ),
    )
    incoming = swap(outgoing, "slab")
    sides = exchange(sides)
    held = double(double(ready, "col", STEPS[0]), "col", STEPS[1])
    held, incoming, sides = lax.optimization_barrier((held, incoming, sides))
    faces = sides
    turned, diag = nnc_trans[0, 0], accum
    field = pressure
    for sweep in range(ITERS_FLOW):
        first = sweep == 0
        last = sweep == ITERS_FLOW - 1
        extra = [] if first else list(faces)
        if last:
            extra += [faults, own, fault_hot]
            outs = [
                (grid[0], F32),
                ((lines, nodes), BF16),
                ((columns, planes, 128), BF16),
            ]
        else:
            outs = [(*grid, 0), ((slabs, lateral, 128), BF16, 0)]
            if first:
                outs += [((slabs, lateral, 128), F32, 0), (*grid, 0)]
            outs += edges
        got = call(
            functools.partial(sweep_kernel, first, last),
            outs,
            incoming,
            turned,
            field,
            source,
            trans_z,
            trans_x,
            trans_y,
            diag,
            cells,
            *sides,
            *extra,
            hbm=(*range(1, 8), *([19] if last else [])),
            scratch=[
                *([] if last else [packet, block]),
                *([values] if first else []),
                *[block] * 6,
                pltpu.VMEM((slabs, lateral, 128), F32),
                values,
                table,
                pltpu.SemaphoreType.DMA((12,)),
            ],
        )
        if last:
            field, fault_hot, whole = got
            break
        field, outgoing = got[:2]
        if first:
            turned, diag = got[2:4]
            held, outgoing = lax.optimization_barrier((held, outgoing))
        else:
            near, far, outgoing = lax.optimization_barrier((near, far, outgoing))
        incoming = swap(outgoing, "slab")
        sides = exchange(got[-4:])
        if first:
            near = double(held, "col", STEPS[2])
            far = paired(near, "col", STEPS[3])
            near, far, incoming, sides = lax.optimization_barrier(
                (near, far, incoming, sides)
            )
        else:
            own, fault_hot = call(
                contact_kernel,
                [((4 * rows, 128), F32), ((lines, nodes), BF16, 0)],
                tile_cols,
                near,
                far,
                blocks,
                base,
                slip0,
                stiff,
                active,
                faults,
                smem=(0,),
                hbm=(3,),
                scratch=(
                    tiles,
                    pltpu.VMEM(blocks.shape, BF16),
                    pltpu.VMEM((lines, nodes), BF16),
                    pltpu.SemaphoreType.DMA((2,)),
                ),
            )
    whole = swap(whole, "col")
    normal, slip, traction = call(
        tail_kernel,
        [((rows, 128), F32), ((3, rows, 128), F32), ((3, rows, 128), F32)],
        tile_cols,
        whole,
        blocks,
        base,
        own,
        stiff,
        active,
        smem=(0,),
        scratch=(pltpu.VMEM((columns * rows, 128), F32), tiles),
    )
    normal = swap(normal.reshape(columns, -1, 128), "col").reshape(columns, 128)
    (pressure_out,) = call(
        back_kernel,
        [grid],
        normal,
        faults,
        fault_hot,
        field,
        diag,
        scratch=(pltpu.VMEM((2 * lateral, nodes), BF16),),
    )
    return (pressure_out, slip.reshape(1, 3, -1), traction.reshape(1, 3, -1))


def solution(mesh):
    return jax.shard_map(
        per_device,
        mesh=mesh,
        in_specs=(
            P("slab", "col", None),
            P("slab", "col", None),
            P("slab", "col", None),
            P("slab", "col", None),
            P("slab", "col", None),
            P("slab", "col", None),
            P("slab", "col", None, None),
            P("slab", "col", None, None, None),
            P("slab", "col", None, None),
            P("slab", None, "col"),
            P("slab", None, "col"),
            P("slab", "col"),
            P(None, "slab", "col"),
            P("slab", "col", None, None, None),
            P("slab", "col", None),
        ),
        out_specs=(P("slab", "col", None), P("slab", None, "col"), P("slab", None, "col")),
        check_vma=False,
    )
```

```python
import functools

import jax
import jax.numpy as jnp
from jax import lax
from jax.experimental import pallas as pl
from jax.experimental.pallas import tpu as pltpu
from jax.sharding import PartitionSpec as P

ITERS_FLOW = 3
BIOT = 0.8
STEPS = (1, 2, 8, 4)
F32 = jnp.float32
BF16 = jnp.bfloat16
NT = (((1,), (1,)), ((), ()))


def call(body, outs, *args, smem=(), hbm=(), scratch=(), mib=14):
    spaces = [
        pltpu.SMEM if i in smem else pltpu.HBM if i in hbm else pltpu.VMEM
        for i in range(len(args))
    ]
    args = [
        pltpu.with_memory_space_constraint(a, pltpu.HBM) if i in hbm else a
        for i, a in enumerate(args)
    ]
    far = [len(o) > 2 for o in outs]
    return pl.pallas_call(
        body,
        in_specs=[pl.BlockSpec(memory_space=space) for space in spaces],
        out_specs=[
            pl.BlockSpec(memory_space=pltpu.HBM if f else pltpu.VMEM) for f in far
        ],
        out_shape=[
            pltpu.HBM(*o[:2]) if f else jax.ShapeDtypeStruct(*o)
            for o, f in zip(outs, far)
        ],
        scratch_shapes=list(scratch),
        compiler_params=pltpu.CompilerParams(vmem_limit_bytes=mib << 20),
    )(*args)


def begin(pairs, sems, at=0):
    copies = [
        pltpu.make_async_copy(source, target, sems.at[at + i])
        for i, (source, target) in enumerate(pairs)
    ]
    for copy in copies:
        copy.start()
    return copies


def finish(copies):
    for copy in copies:
        copy.wait()


def iota(shape, dim):
    return lax.broadcasted_iota(jnp.int32, shape, dim)


def halves(x):
    high = x.astype(BF16)
    return high, (x - high.astype(F32)).astype(BF16)


def fill_hot(hot_ref, lines, width):
    depth = hot_ref.shape[0] // width
    shift = width.bit_length() - 1
    for q in range(lines.shape[0]):
        line = lines[q : q + 1, :]
        layer = jnp.broadcast_to(line >> shift, (16, 128))
        place = jnp.where(iota((width, 128), 0) == line & (width - 1), 1.0, 0.0).astype(BF16)
        for i in range(depth):
            here = jnp.where(layer == i, 1.0, 0.0).astype(BF16)
            for j in range(0, width, 16):
                hot_ref[i * width + j : i * width + j + 16, q * 128 : (q + 1) * 128] = (
                    place[j : j + 16] * here
                )


def gather_lines(hot_ref, field, out_ref):
    turned = field.T.astype(BF16)
    for q in range(0, out_ref.shape[0], 2):
        got = jnp.dot(
            turned, hot_ref[:, q * 128 : (q + 2) * 128], preferred_element_type=F32
        ).astype(BF16)
        out_ref[q] = got[:, :128]
        out_ref[q + 1] = got[:, 128:]


def scatter_lines(hot_ref, values_ref):
    both = lax.dot_general(hot_ref[...], values_ref[...], NT, preferred_element_type=F32)
    return both[:, :128] + both[:, 128:]


def put_halves(values_ref, q, values):
    high, low = halves(values)
    values_ref[:128, q * 128 : (q + 1) * 128] = high
    values_ref[128:, q * 128 : (q + 1) * 128] = low


def odd(axis):
    return lax.axis_index(axis) % 2 == 1


def put_edges(field_ref, edge_refs):
    z_one, z_two, x_one, x_two = edge_refs
    depth, width, _ = field_ref.shape
    swap_z, swap_x = odd("slab"), odd("col")
    head, tail = field_ref[0], field_ref[depth - 1]
    z_one[0] = jnp.where(swap_z, head, tail).astype(BF16)
    z_two[0] = jnp.where(swap_z, tail, head).astype(BF16)
    heads = jnp.concatenate([field_ref[i, 0:1, :] for i in range(depth)], 0)
    tails = jnp.concatenate(
        [field_ref[i, width - 1 : width, :] for i in range(depth)], 0
    )
    x_one[0] = jnp.where(swap_x, heads, tails).astype(BF16)
    x_two[0] = jnp.where(swap_x, tails, heads).astype(BF16)


def first_kernel(
    field_hbm,
    face_z_hbm,
    face_x_hbm,
    slip_hbm,
    cell_ref,
    out_hbm,
    ready_ref,
    kept_ref,
    z_one,
    z_two,
    x_one,
    x_two,
    hot_ref,
    field_ref,
    wall_ref,
    layer_ref,
    slip_ref,
    out_ref,
    sems,
):
    depth, width, lateral = field_ref.shape
    reads = begin(
        [
            (field_hbm, field_ref),
            (face_x_hbm.at[:, pl.ds(width - 8, 8), :], wall_ref),
            (face_z_hbm.at[depth - 1], layer_ref),
            (slip_hbm, slip_ref),
        ],
        sems,
    )
    kept_ref[...] = cell_ref[...]
    fill_hot(hot_ref, cell_ref[...], width)
    finish(reads)
    gather_lines(hot_ref, field_ref[...].reshape(depth * width, lateral), out_ref)
    writes = begin([(out_ref, out_hbm)], sems, 4)
    parts, rows, _ = slip_ref.shape
    for p in range(parts):
        ready_ref[0, p * rows : (p + 1) * rows, :] = slip_ref[p].astype(BF16)
    put_edges(field_ref, (z_one, z_two, x_one, x_two))
    layer = layer_ref[...].astype(BF16)
    wall = jnp.concatenate([wall_ref[i, 7:8, :] for i in range(depth)], 0).astype(BF16)
    z_one[1] = layer
    z_two[1] = layer
    x_one[1] = wall
    x_two[1] = wall
    finish(writes)


def pick(choice, one, two):
    return jnp.where(choice, one.astype(F32), two.astype(F32))


def sweep_kernel(
    first,
    last,
    incoming_ref,
    turned_hbm,
    field_hbm,
    source_hbm,
    face_z_hbm,
    face_x_hbm,
    face_y_hbm,
    diag_hbm,
    cell_ref,
    z_one,
    z_two,
    x_one,
    x_two,
    *refs,
):
    refs = list(refs)
    sems = refs.pop()
    hot_ref, values_ref, turned_ref = [refs.pop() for _ in range(3)]
    big = [refs.pop() for _ in range(6)]
    field_ref, source_ref, face_z_ref, face_x_ref, face_y_ref, diag_ref = big
    depth, width, lateral = field_ref.shape
    if first:
        link_ref = refs.pop()
    if not last:
        new_ref, out_ref = refs.pop(), refs.pop()
    faces = [z_one, z_two, x_one, x_two] if first else [refs.pop(0) for _ in range(4)]
    linked_reads = begin([(turned_hbm, turned_ref)], sems)
    reads = begin(
        list(
            zip(
                (field_hbm, source_hbm, face_z_hbm, face_x_hbm, face_y_hbm, diag_hbm),
                big,
            )
        ),
        sems,
        2,
    )
    if last:
        table_reads = begin([(refs[2], refs[4])], sems, 8)
    fill_hot(hot_ref, cell_ref[...], width)
    finish(linked_reads)
    for q in range(incoming_ref.shape[0]):
        turned = turned_ref[q]
        if first:
            turned = turned.T
            turned_ref[q] = turned
            put_halves(link_ref, q, turned)
        put_halves(values_ref, q, turned * incoming_ref[q].astype(F32))
    linked = scatter_lines(hot_ref, values_ref)
    if first:
        conduct = scatter_lines(hot_ref, link_ref)
        last_z = lax.axis_index("slab") == lax.axis_size("slab") - 1
        last_x = lax.axis_index("col") == lax.axis_size("col") - 1
    finish(reads)
    writes = []
    if last:
        fault_ref, own_ref, _, new_ref, fault_hot_ref, press_ref = refs
    elif first:
        new_hbm, out_hbm, turned_out, inverse_out = refs[:4]
        edge_refs = refs[4:]
        writes += begin([(turned_ref, turned_out)], sems, 8)
    else:
        new_hbm, out_hbm = refs[:2]
        edge_refs = refs[2:]
    swap_z, swap_x = odd("slab"), odd("col")
    below_z = pick(swap_z, z_one[0], z_two[0])
    above_z = pick(swap_z, z_two[0], z_one[0])
    edge_z = pick(swap_z, faces[0][1], faces[1][1])
    behind_x = pick(swap_x, x_one[0], x_two[0])
    ahead_x = pick(swap_x, x_two[0], x_one[0])
    edge_x = pick(swap_x, faces[2][1], faces[3][1])
    across = iota((width, lateral), 0)
    along = iota((width, lateral), 1)
    for i in range(depth):
        field = field_ref[i]
        face_z = face_z_ref[i]
        lower_z = face_z_ref[i - 1] if i > 0 else edge_z
        above = field_ref[i + 1] if i < depth - 1 else above_z
        below = field_ref[i - 1] if i > 0 else below_z
        total = source_ref[i] + linked[i * width : (i + 1) * width]
        total = total + face_z * above + lower_z * below
        face_x = face_x_ref[i]
        lower_x = edge_x[i : i + 1, :]
        ahead = jnp.where(
            across == width - 1, ahead_x[i : i + 1, :], pltpu.roll(field, width - 1, 0)
        )
        flow = jnp.where(
            across == 0,
            lower_x * behind_x[i : i + 1, :],
            pltpu.roll(face_x * field, 1, 0),
        )
        total = total + face_x * ahead + flow
        face_y = jnp.where(along == lateral - 1, 0.0, face_y_ref[i])
        total = total + face_y * pltpu.roll(field, lateral - 1, 1)
        total = total + pltpu.roll(face_y * field, 1, 1)
        if first:
            whole = diag_ref[i] + conduct[i * width : (i + 1) * width] + lower_z
            own_z = jnp.where(last_z, 0.0, face_z) if i == depth - 1 else face_z
            whole = whole + own_z + face_y + pltpu.roll(face_y, 1, 1)
            whole = whole + jnp.where((across == width - 1) & last_x, 0.0, face_x)
            whole = whole + jnp.where(across == 0, lower_x, pltpu.roll(face_x, 1, 0))
            inverse = 1.0 / whole
            diag_ref[i] = inverse
        else:
            inverse = diag_ref[i]
        new_ref[i] = total * inverse
    lines = new_ref[...].reshape(depth * width, lateral)
    if last:
        finish(table_reads)
        high, low = halves(lines.T)
        both = jnp.concatenate([high, low], 0)
        side = iota((lateral, 128), 0)
        for q in range(0, fault_ref.shape[0], 2):
            pair = jnp.dot(
                both, fault_hot_ref[:, q * 128 : (q + 2) * 128], preferred_element_type=F32
            )
            pair = pair[:lateral] + pair[lateral:]
            for n in (0, 1):
                lane = fault_ref[q + n : q + n + 1, :] & 127
                got = pair[:, n * 128 : (n + 1) * 128]
                got = jnp.sum(jnp.where(side == lane, got, 0.0), 0, keepdims=True)
                face_x_ref[0, q + n : q + n + 1, :] = got
        rows = fault_ref.shape[0]
        planes = [
            *halves(face_x_ref[0, :rows, :]),
            *halves(own_ref[:rows]),
            *[own_ref[n * rows : (n + 1) * rows].astype(BF16) for n in (1, 2, 3)],
        ]
        for n, plane in enumerate(planes):
            press_ref[0, n * rows : (n + 1) * rows, :] = plane
        mine = press_ref[0]
        for o in range(1, press_ref.shape[0]):
            press_ref[o] = mine
    else:
        writes += begin([(new_ref, new_hbm)], sems, 9)
        if first:
            writes += begin([(diag_ref, inverse_out)], sems, 10)
        gather_lines(hot_ref, lines, out_ref)
        writes += begin([(out_ref, out_hbm)], sems, 11)
        put_edges(new_ref, edge_refs)
    finish(writes)


def couple(cols_ref, tiles_ref, blocks_ref):
    rows, per = blocks_ref.shape[:2]
    ids = iota((rows, 128), 0)
    total = None
    for r in range(rows):
        for b in range(per):
            at = pl.ds(cols_ref[r, b], 1)
            left = [
                jnp.where(ids == r, tiles_ref[p, at, :], 0.0)
                for p in range(tiles_ref.shape[0])
            ]
            left = jnp.concatenate(left, 0).astype(BF16)
            part = lax.dot_general(left, blocks_ref[r, b], NT, preferred_element_type=F32)
            total = part if total is None else total + part
    return total


def contact_kernel(
    width,
    cols_ref,
    near_ref,
    far_ref,
    blocks_hbm,
    base_ref,
    slip_ref,
    stiff_ref,
    active_ref,
    fault_ref,
    own_ref,
    fault_hot_hbm,
    tiles_ref,
    blocks_ref,
    fault_hot_ref,
    sems,
):
    reads = begin([(blocks_hbm, blocks_ref)], sems)
    fill_hot(fault_hot_ref, fault_ref[...] >> 7, width)
    writes = begin([(fault_hot_ref, fault_hot_hbm)], sems, 1)
    rows = base_ref.shape[1]
    me = lax.axis_index("col")
    held = near_ref.shape[0]
    for n in range(2 * held):
        apart = sum(bit for k, bit in enumerate(STEPS) if n >> k & 1)
        owner = pl.multiple_of((me ^ apart) * rows, rows)
        for p in range(3):
            ref = near_ref if n < held else far_ref
            part = ref[n % held, p * rows : (p + 1) * rows, :].astype(F32)
            tiles_ref[p, pl.ds(owner, rows), :] = part
    finish(reads)
    coupled = couple(cols_ref, tiles_ref, blocks_ref)
    gain = active_ref[0].astype(F32) / stiff_ref[...]
    parts = [
        slip_ref[p] + gain * (base_ref[p] - coupled[p * rows : (p + 1) * rows])
        for p in range(3)
    ]
    own_ref[...] = jnp.concatenate([parts[0], -BIOT * gain, parts[1], parts[2]], 0)
    finish(writes)


def tail_kernel(
    cols_ref,
    whole_ref,
    blocks_ref,
    base_ref,
    own_ref,
    stiff_ref,
    active_ref,
    normal_ref,
    slip_ref,
    traction_ref,
    press_ref,
    tiles_ref,
):
    sources = whole_ref.shape[0]
    rows = base_ref.shape[1]
    ids = sources * rows
    def part(n):
        plane = whole_ref[:, n * rows : (n + 1) * rows, :].astype(F32)
        return plane.reshape(ids, 128)

    for c in range(sources):
        press = whole_ref[c, :rows, :].astype(F32) + whole_ref[c, rows : 2 * rows, :]
        press_ref[pl.ds(c, sources, stride=rows), :] = press
    slips = [part(2) + part(3) + part(4) * press_ref[...], part(5), part(6)]
    for p in range(3):
        tiles_ref[p] = slips[p].astype(BF16).astype(F32)
    coupled = couple(cols_ref, tiles_ref, blocks_ref)
    mine = press_ref[pl.ds(pl.multiple_of(lax.axis_index("col") * rows, rows), rows), :]
    gain = active_ref[1].astype(F32) / stiff_ref[...]
    own = [own_ref[n * rows : (n + 1) * rows] for n in range(4)]
    slips = [own[0] + own[1] * mine, own[2], own[3]]
    loads = [base_ref[0] - BIOT * mine, base_ref[1], base_ref[2]]
    for p in range(3):
        traction = loads[p] - coupled[p * rows : (p + 1) * rows]
        traction_ref[p] = traction
        slip_ref[p] = slips[p] + gain * traction
        if p == 0:
            normal_ref[...] = traction


def back_kernel(
    normal_ref, fault_ref, fault_hot_ref, field_ref, inverse_ref, out_ref, values_ref
):
    depth, width, lateral = field_ref.shape
    side = iota((lateral, 128), 0)
    for q in range(normal_ref.shape[0]):
        lane = fault_ref[q : q + 1, :] & 127
        put_halves(values_ref, q, jnp.where(side == lane, normal_ref[q : q + 1, :], 0.0))
    returned = scatter_lines(fault_hot_ref, values_ref).reshape(depth, width, lateral)
    out_ref[...] = field_ref[...] + returned * inverse_ref[...]


def exchange(edges):
    got = []
    for edge, (axis, start) in zip(edges, (("slab", 0), ("slab", 1), ("col", 0), ("col", 1))):
        count = lax.axis_size(axis)
        pairs = [(i, i + 1) for i in range(start, count - 1, 2)]
        got.append(lax.ppermute(edge, axis, pairs + [(j, i) for i, j in pairs]))
    return got


def paired(block, axis, apart):
    return lax.ppermute(block, axis, [(i, i ^ apart) for i in range(lax.axis_size(axis))])


def double(block, axis, apart):
    return jnp.concatenate([block, paired(block, axis, apart)], 0)


def swap(blocks, axis):
    return lax.all_to_all(blocks, axis, split_axis=0, concat_axis=0, tiled=True)


def per_device(
    pressure,
    source,
    accum,
    trans_z,
    trans_x,
    trans_y,
    nnc_cell,
    nnc_trans,
    fault_cell,
    base_stress,
    slip_start,
    stiff_diag,
    active_set,
    mortar_blocks,
    mortar_cols,
):
    depth, width, lateral = pressure.shape
    slabs = lax.axis_size("slab")
    columns = lax.axis_size("col")
    lines = depth * width
    grid = ((depth, width, lateral), F32)
    slots = slabs * 128
    nodes = columns * 128
    rows = mortar_blocks.shape[1]
    cells = nnc_cell[0, 0]
    faults = fault_cell[0, 0]
    blocks = mortar_blocks[0]
    tile_cols = mortar_cols[0]
    base = base_stress[0].reshape(3, rows, 128)
    slip0 = slip_start[0].reshape(3, rows, 128)
    stiff = stiff_diag[0].reshape(rows, 128)
    active = active_set[:, 0].reshape(-1, rows, 128)
    tiles = pltpu.VMEM((3, columns * rows, 128), F32)
    layer, wall = (width, lateral), (depth, lateral)
    table = pltpu.VMEM((lines, slots), BF16)
    block = pltpu.VMEM((depth, width, lateral), F32)
    packet = pltpu.VMEM((slabs, lateral, 128), BF16)
    values = pltpu.VMEM((2 * lateral, slots), BF16)
    edges = [((1, *layer), BF16)] * 2 + [((1, *wall), BF16)] * 2
    doubled = [((2, *layer), BF16)] * 2 + [((2, *wall), BF16)] * 2
    planes = 7 * rows

    outgoing, ready, cells, *sides = call(
        first_kernel,
        [
            ((slabs, lateral, 128), BF16, 0),
            ((1, 3 * rows, 128), BF16),
            (cells.shape, jnp.int32),
            *doubled,
        ],
        pressure,
        trans_z,
        trans_x,
        slip0,
        cells,
        hbm=(0, 1, 2, 3),
        scratch=(
            table,
            block,
            pltpu.VMEM((depth, 8, lateral), F32),
            pltpu.VMEM(layer, F32),
            pltpu.VMEM(slip0.shape, F32),
            packet,
            pltpu.SemaphoreType.DMA((5,)),
        ),
    )
    incoming = swap(outgoing, "slab")
    sides = exchange(sides)
    held = double(double(ready, "col", STEPS[0]), "col", STEPS[1])
    held, incoming, sides = lax.optimization_barrier((held, incoming, sides))
    faces = sides
    turned, diag = nnc_trans[0, 0], accum
    field = pressure
    for sweep in range(ITERS_FLOW):
        first = sweep == 0
        last = sweep == ITERS_FLOW - 1
        extra = [] if first else list(faces)
        if last:
            extra += [faults, own, fault_hot]
            outs = [
                (grid[0], F32),
                ((lines, nodes), BF16),
                ((columns, planes, 128), BF16),
            ]
        else:
            outs = [(*grid, 0), ((slabs, lateral, 128), BF16, 0)]
            if first:
                outs += [((slabs, lateral, 128), F32, 0), (*grid, 0)]
            outs += edges
        got = call(
            functools.partial(sweep_kernel, first, last),
            outs,
            incoming,
            turned,
            field,
            source,
            trans_z,
            trans_x,
            trans_y,
            diag,
            cells,
            *sides,
            *extra,
            hbm=(*range(1, 8), *([19] if last else [])),
            scratch=[
                *([] if last else [packet, block]),
                *([values] if first else []),
                *[block] * 6,
                pltpu.VMEM((slabs, lateral, 128), F32),
                values,
                table,
                pltpu.SemaphoreType.DMA((12,)),
            ],
        )
        if last:
            field, fault_hot, whole = got
            break
        field, outgoing = got[:2]
        if first:
            turned, diag = got[2:4]
            held, outgoing = lax.optimization_barrier((held, outgoing))
        else:
            held, other, outgoing = lax.optimization_barrier((held, other, outgoing))
        incoming = swap(outgoing, "slab")
        sides = exchange(got[-4:])
        if first:
            other = paired(held, "col", STEPS[2])
            other, incoming, sides = lax.optimization_barrier((other, incoming, sides))
        else:
            near = jnp.concatenate([held, other], 0)
            far = paired(near, "col", STEPS[3])
            own, fault_hot = call(
                functools.partial(contact_kernel, width),
                [((4 * rows, 128), F32), ((lines, nodes), BF16, 0)],
                tile_cols,
                near,
                far,
                blocks,
                base,
                slip0,
                stiff,
                active,
                faults,
                smem=(0,),
                hbm=(3,),
                scratch=(
                    tiles,
                    pltpu.VMEM(blocks.shape, BF16),
                    pltpu.VMEM((lines, nodes), BF16),
                    pltpu.SemaphoreType.DMA((2,)),
                ),
            )
    whole = swap(whole, "col")
    normal, slip, traction = call(
        tail_kernel,
        [((rows, 128), F32), ((3, rows, 128), F32), ((3, rows, 128), F32)],
        tile_cols,
        whole,
        blocks,
        base,
        own,
        stiff,
        active,
        smem=(0,),
        scratch=(pltpu.VMEM((columns * rows, 128), F32), tiles),
    )
    normal = swap(normal.reshape(columns, -1, 128), "col").reshape(columns, 128)
    (pressure_out,) = call(
        back_kernel,
        [grid],
        normal,
        faults,
        fault_hot,
        field,
        diag,
        scratch=(pltpu.VMEM((2 * lateral, nodes), BF16),),
    )
    return (pressure_out, slip.reshape(1, 3, -1), traction.reshape(1, 3, -1))


def solution(mesh):
    return jax.shard_map(
        per_device,
        mesh=mesh,
        in_specs=(
            P("slab", "col", None),
            P("slab", "col", None),
            P("slab", "col", None),
            P("slab", "col", None),
            P("slab", "col", None),
            P("slab", "col", None),
            P("slab", "col", None, None),
            P("slab", "col", None, None, None),
            P("slab", "col", None, None),
            P("slab", None, "col"),
            P("slab", None, "col"),
            P("slab", "col"),
            P(None, "slab", "col"),
            P("slab", "col", None, None, None),
            P("slab", "col", None),
        ),
        out_specs=(P("slab", "col", None), P("slab", None, "col"), P("slab", None, "col")),
        check_vma=False,
    )
```

```python
import functools

import jax
import jax.numpy as jnp
from jax import lax
from jax.experimental import pallas as pl
from jax.experimental.pallas import tpu as pltpu
from jax.sharding import PartitionSpec as P

ITERS_FLOW = 3
BIOT = 0.8
STEPS = (1, 2, 8, 4)
F32 = jnp.float32
BF16 = jnp.bfloat16
NT = (((1,), (1,)), ((), ()))


def call(body, outs, *args, smem=(), hbm=(), scratch=(), mib=14):
    spaces = [
        pltpu.SMEM if i in smem else pltpu.HBM if i in hbm else pltpu.VMEM
        for i in range(len(args))
    ]
    args = [
        pltpu.with_memory_space_constraint(a, pltpu.HBM) if i in hbm else a
        for i, a in enumerate(args)
    ]
    far = [len(o) > 2 for o in outs]
    return pl.pallas_call(
        body,
        in_specs=[pl.BlockSpec(memory_space=space) for space in spaces],
        out_specs=[
            pl.BlockSpec(memory_space=pltpu.HBM if f else pltpu.VMEM) for f in far
        ],
        out_shape=[
            pltpu.HBM(*o[:2]) if f else jax.ShapeDtypeStruct(*o)
            for o, f in zip(outs, far)
        ],
        scratch_shapes=list(scratch),
        compiler_params=pltpu.CompilerParams(vmem_limit_bytes=mib << 20),
    )(*args)


def begin(pairs, sems, at=0):
    copies = [
        pltpu.make_async_copy(source, target, sems.at[at + i])
        for i, (source, target) in enumerate(pairs)
    ]
    for copy in copies:
        copy.start()
    return copies


def finish(copies):
    for copy in copies:
        copy.wait()


def iota(shape, dim):
    return lax.broadcasted_iota(jnp.int32, shape, dim)


def halves(x):
    high = x.astype(BF16)
    return high, (x - high.astype(F32)).astype(BF16)


def fill_hot(hot_ref, lines, width):
    depth = hot_ref.shape[0] // width
    shift = width.bit_length() - 1
    for q in range(lines.shape[0]):
        line = lines[q : q + 1, :]
        layer = jnp.broadcast_to(line >> shift, (16, 128))
        place = jnp.where(iota((width, 128), 0) == line & (width - 1), 1.0, 0.0).astype(BF16)
        for i in range(depth):
            here = jnp.where(layer == i, 1.0, 0.0).astype(BF16)
            for j in range(0, width, 16):
                hot_ref[i * width + j : i * width + j + 16, q * 128 : (q + 1) * 128] = (
                    place[j : j + 16] * here
                )


def gather_lines(hot_ref, field, out_ref, out_hbm, sems, at):
    turned = field.T.astype(BF16)
    copies = []
    for q in range(0, out_ref.shape[0], 2):
        got = jnp.dot(
            turned, hot_ref[:, q * 128 : (q + 2) * 128], preferred_element_type=F32
        ).astype(BF16)
        out_ref[q] = got[:, :128]
        out_ref[q + 1] = got[:, 128:]
        pair = pl.ds(q, 2)
        copies += begin([(out_ref.at[pair], out_hbm.at[pair])], sems, at + q // 2)
    return copies


def scatter_lines(hot_ref, values_ref):
    both = lax.dot_general(hot_ref[...], values_ref[...], NT, preferred_element_type=F32)
    return both[:, :128] + both[:, 128:]


def put_halves(values_ref, q, values):
    high, low = halves(values)
    values_ref[:128, q * 128 : (q + 1) * 128] = high
    values_ref[128:, q * 128 : (q + 1) * 128] = low


def odd(axis):
    return lax.axis_index(axis) % 2 == 1


def put_edges(field_ref, edge_refs):
    z_one, z_two, x_one, x_two = edge_refs
    depth, width, _ = field_ref.shape
    swap_z, swap_x = odd("slab"), odd("col")
    head, tail = field_ref[0], field_ref[depth - 1]
    z_one[0] = jnp.where(swap_z, head, tail).astype(BF16)
    z_two[0] = jnp.where(swap_z, tail, head).astype(BF16)
    heads = jnp.concatenate([field_ref[i, 0:1, :] for i in range(depth)], 0)
    tails = jnp.concatenate(
        [field_ref[i, width - 1 : width, :] for i in range(depth)], 0
    )
    x_one[0] = jnp.where(swap_x, heads, tails).astype(BF16)
    x_two[0] = jnp.where(swap_x, tails, heads).astype(BF16)


def first_kernel(
    field_hbm,
    face_z_hbm,
    face_x_hbm,
    slip_hbm,
    cell_ref,
    out_hbm,
    ready_ref,
    kept_ref,
    z_one,
    z_two,
    x_one,
    x_two,
    hot_ref,
    field_ref,
    wall_ref,
    layer_ref,
    slip_ref,
    out_ref,
    sems,
):
    depth, width, lateral = field_ref.shape
    reads = begin(
        [
            (field_hbm, field_ref),
            (face_x_hbm.at[:, pl.ds(width - 8, 8), :], wall_ref),
            (face_z_hbm.at[depth - 1], layer_ref),
            (slip_hbm, slip_ref),
        ],
        sems,
    )
    kept_ref[...] = cell_ref[...]
    fill_hot(hot_ref, cell_ref[...], width)
    finish(reads)
    lines = field_ref[...].reshape(depth * width, lateral)
    writes = gather_lines(hot_ref, lines, out_ref, out_hbm, sems, 4)
    parts, rows, _ = slip_ref.shape
    for p in range(parts):
        ready_ref[0, p * rows : (p + 1) * rows, :] = slip_ref[p].astype(BF16)
    put_edges(field_ref, (z_one, z_two, x_one, x_two))
    layer = layer_ref[...].astype(BF16)
    wall = jnp.concatenate([wall_ref[i, 7:8, :] for i in range(depth)], 0).astype(BF16)
    z_one[1] = layer
    z_two[1] = layer
    x_one[1] = wall
    x_two[1] = wall
    finish(writes)


def pick(choice, one, two):
    return jnp.where(choice, one.astype(F32), two.astype(F32))


def sweep_kernel(
    first,
    last,
    incoming_ref,
    turned_hbm,
    field_hbm,
    source_hbm,
    face_z_hbm,
    face_x_hbm,
    face_y_hbm,
    diag_hbm,
    cell_ref,
    z_one,
    z_two,
    x_one,
    x_two,
    *refs,
):
    refs = list(refs)
    sems = refs.pop()
    hot_ref, values_ref, turned_ref = [refs.pop() for _ in range(3)]
    big = [refs.pop() for _ in range(6)]
    field_ref, source_ref, face_z_ref, face_x_ref, face_y_ref, diag_ref = big
    depth, width, lateral = field_ref.shape
    if first:
        link_ref = refs.pop()
    if not last:
        new_ref, out_ref = refs.pop(), refs.pop()
    faces = [z_one, z_two, x_one, x_two] if first else [refs.pop(0) for _ in range(4)]
    linked_reads = begin([(turned_hbm, turned_ref)], sems)
    fill_hot(hot_ref, cell_ref[...], width)
    finish(linked_reads)
    reads = begin(
        list(
            zip(
                (field_hbm, source_hbm, face_z_hbm, face_x_hbm, face_y_hbm, diag_hbm),
                big,
            )
        ),
        sems,
        2,
    )
    if last:
        table_reads = begin([(refs[2], refs[4])], sems, 8)
    for q in range(incoming_ref.shape[0]):
        turned = turned_ref[q]
        if first:
            turned = turned.T
            turned_ref[q] = turned
            put_halves(link_ref, q, turned)
        put_halves(values_ref, q, turned * incoming_ref[q].astype(F32))
    linked = scatter_lines(hot_ref, values_ref)
    if first:
        conduct = scatter_lines(hot_ref, link_ref)
        last_z = lax.axis_index("slab") == lax.axis_size("slab") - 1
        last_x = lax.axis_index("col") == lax.axis_size("col") - 1
    finish(reads)
    writes = []
    if last:
        fault_ref, own_ref, _, new_ref, fault_hot_ref, press_ref = refs
    elif first:
        new_hbm, out_hbm, turned_out, inverse_out = refs[:4]
        edge_refs = refs[4:]
        writes += begin([(turned_ref, turned_out)], sems, 8)
    else:
        new_hbm, out_hbm = refs[:2]
        edge_refs = refs[2:]
    swap_z, swap_x = odd("slab"), odd("col")
    below_z = pick(swap_z, z_one[0], z_two[0])
    above_z = pick(swap_z, z_two[0], z_one[0])
    edge_z = pick(swap_z, faces[0][1], faces[1][1])
    behind_x = pick(swap_x, x_one[0], x_two[0])
    ahead_x = pick(swap_x, x_two[0], x_one[0])
    edge_x = pick(swap_x, faces[2][1], faces[3][1])
    across = iota((width, lateral), 0)
    along = iota((width, lateral), 1)
    for i in range(depth):
        field = field_ref[i]
        face_z = face_z_ref[i]
        lower_z = face_z_ref[i - 1] if i > 0 else edge_z
        above = field_ref[i + 1] if i < depth - 1 else above_z
        below = field_ref[i - 1] if i > 0 else below_z
        total = source_ref[i] + linked[i * width : (i + 1) * width]
        total = total + face_z * above + lower_z * below
        face_x = face_x_ref[i]
        lower_x = edge_x[i : i + 1, :]
        ahead = jnp.where(
            across == width - 1, ahead_x[i : i + 1, :], pltpu.roll(field, width - 1, 0)
        )
        flow = jnp.where(
            across == 0,
            lower_x * behind_x[i : i + 1, :],
            pltpu.roll(face_x * field, 1, 0),
        )
        total = total + face_x * ahead + flow
        face_y = jnp.where(along == lateral - 1, 0.0, face_y_ref[i])
        total = total + face_y * pltpu.roll(field, lateral - 1, 1)
        total = total + pltpu.roll(face_y * field, 1, 1)
        if first:
            whole = diag_ref[i] + conduct[i * width : (i + 1) * width] + lower_z
            own_z = jnp.where(last_z, 0.0, face_z) if i == depth - 1 else face_z
            whole = whole + own_z + face_y + pltpu.roll(face_y, 1, 1)
            whole = whole + jnp.where((across == width - 1) & last_x, 0.0, face_x)
            whole = whole + jnp.where(across == 0, lower_x, pltpu.roll(face_x, 1, 0))
            inverse = 1.0 / whole
            diag_ref[i] = inverse
        else:
            inverse = diag_ref[i]
        new_ref[i] = total * inverse
    lines = new_ref[...].reshape(depth * width, lateral)
    if last:
        finish(table_reads)
        high, low = halves(lines.T)
        both = jnp.concatenate([high, low], 0)
        side = iota((lateral, 128), 0)
        for q in range(0, fault_ref.shape[0], 2):
            pair = jnp.dot(
                both, fault_hot_ref[:, q * 128 : (q + 2) * 128], preferred_element_type=F32
            )
            pair = pair[:lateral] + pair[lateral:]
            for n in (0, 1):
                lane = fault_ref[q + n : q + n + 1, :] & 127
                got = pair[:, n * 128 : (n + 1) * 128]
                got = jnp.sum(jnp.where(side == lane, got, 0.0), 0, keepdims=True)
                face_x_ref[0, q + n : q + n + 1, :] = got
        rows = fault_ref.shape[0]
        planes = [
            *halves(face_x_ref[0, :rows, :]),
            *halves(own_ref[:rows]),
            *[own_ref[n * rows : (n + 1) * rows].astype(BF16) for n in (1, 2, 3)],
        ]
        for n, plane in enumerate(planes):
            press_ref[0, n * rows : (n + 1) * rows, :] = plane
        mine = press_ref[0]
        for o in range(1, press_ref.shape[0]):
            press_ref[o] = mine
    else:
        writes += begin([(new_ref, new_hbm)], sems, 9)
        if first:
            writes += begin([(diag_ref, inverse_out)], sems, 10)
        writes += gather_lines(hot_ref, lines, out_ref, out_hbm, sems, 11)
        put_edges(new_ref, edge_refs)
    finish(writes)


def couple(cols_ref, tiles_ref, blocks_ref):
    rows, per = blocks_ref.shape[:2]
    ids = iota((rows, 128), 0)
    total = None
    for r in range(rows):
        for b in range(per):
            at = pl.ds(cols_ref[r, b], 1)
            left = [
                jnp.where(ids == r, tiles_ref[p, at, :], 0.0)
                for p in range(tiles_ref.shape[0])
            ]
            left = jnp.concatenate(left, 0).astype(BF16)
            part = lax.dot_general(left, blocks_ref[r, b], NT, preferred_element_type=F32)
            total = part if total is None else total + part
    return total


def contact_kernel(
    width,
    cols_ref,
    near_ref,
    far_ref,
    blocks_hbm,
    base_ref,
    slip_ref,
    stiff_ref,
    active_ref,
    fault_ref,
    own_ref,
    fault_hot_hbm,
    tiles_ref,
    blocks_ref,
    fault_hot_ref,
    sems,
):
    reads = begin([(blocks_hbm, blocks_ref)], sems)
    fill_hot(fault_hot_ref, fault_ref[...] >> 7, width)
    writes = begin([(fault_hot_ref, fault_hot_hbm)], sems, 1)
    rows = base_ref.shape[1]
    me = lax.axis_index("col")
    held = near_ref.shape[0]
    for n in range(2 * held):
        apart = sum(bit for k, bit in enumerate(STEPS) if n >> k & 1)
        owner = pl.multiple_of((me ^ apart) * rows, rows)
        for p in range(3):
            ref = near_ref if n < held else far_ref
            part = ref[n % held, p * rows : (p + 1) * rows, :].astype(F32)
            tiles_ref[p, pl.ds(owner, rows), :] = part
    finish(reads)
    coupled = couple(cols_ref, tiles_ref, blocks_ref)
    gain = active_ref[0].astype(F32) / stiff_ref[...]
    parts = [
        slip_ref[p] + gain * (base_ref[p] - coupled[p * rows : (p + 1) * rows])
        for p in range(3)
    ]
    own_ref[...] = jnp.concatenate([parts[0], -BIOT * gain, parts[1], parts[2]], 0)
    finish(writes)


def tail_kernel(
    cols_ref,
    whole_ref,
    blocks_ref,
    base_ref,
    own_ref,
    stiff_ref,
    active_ref,
    normal_ref,
    slip_ref,
    traction_ref,
    press_ref,
    tiles_ref,
):
    sources = whole_ref.shape[0]
    rows = base_ref.shape[1]
    ids = sources * rows
    def part(n):
        plane = whole_ref[:, n * rows : (n + 1) * rows, :].astype(F32)
        return plane.reshape(ids, 128)

    for c in range(sources):
        press = whole_ref[c, :rows, :].astype(F32) + whole_ref[c, rows : 2 * rows, :]
        press_ref[pl.ds(c, sources, stride=rows), :] = press
    slips = [part(2) + part(3) + part(4) * press_ref[...], part(5), part(6)]
    for p in range(3):
        tiles_ref[p] = slips[p].astype(BF16).astype(F32)
    coupled = couple(cols_ref, tiles_ref, blocks_ref)
    mine = press_ref[pl.ds(pl.multiple_of(lax.axis_index("col") * rows, rows), rows), :]
    gain = active_ref[1].astype(F32) / stiff_ref[...]
    own = [own_ref[n * rows : (n + 1) * rows] for n in range(4)]
    slips = [own[0] + own[1] * mine, own[2], own[3]]
    loads = [base_ref[0] - BIOT * mine, base_ref[1], base_ref[2]]
    for p in range(3):
        traction = loads[p] - coupled[p * rows : (p + 1) * rows]
        traction_ref[p] = traction
        slip_ref[p] = slips[p] + gain * traction
        if p == 0:
            normal_ref[...] = traction


def back_kernel(
    normal_ref, fault_ref, fault_hot_ref, field_ref, inverse_ref, out_ref, values_ref
):
    depth, width, lateral = field_ref.shape
    side = iota((lateral, 128), 0)
    for q in range(normal_ref.shape[0]):
        lane = fault_ref[q : q + 1, :] & 127
        put_halves(values_ref, q, jnp.where(side == lane, normal_ref[q : q + 1, :], 0.0))
    returned = scatter_lines(fault_hot_ref, values_ref).reshape(depth, width, lateral)
    out_ref[...] = field_ref[...] + returned * inverse_ref[...]


def exchange(edges):
    got = []
    for edge, (axis, start) in zip(edges, (("slab", 0), ("slab", 1), ("col", 0), ("col", 1))):
        count = lax.axis_size(axis)
        pairs = [(i, i + 1) for i in range(start, count - 1, 2)]
        got.append(lax.ppermute(edge, axis, pairs + [(j, i) for i, j in pairs]))
    return got


def paired(block, axis, apart):
    return lax.ppermute(block, axis, [(i, i ^ apart) for i in range(lax.axis_size(axis))])


def double(block, axis, apart):
    return jnp.concatenate([block, paired(block, axis, apart)], 0)


def swap(blocks, axis):
    return lax.all_to_all(blocks, axis, split_axis=0, concat_axis=0, tiled=True)


def per_device(
    pressure,
    source,
    accum,
    trans_z,
    trans_x,
    trans_y,
    nnc_cell,
    nnc_trans,
    fault_cell,
    base_stress,
    slip_start,
    stiff_diag,
    active_set,
    mortar_blocks,
    mortar_cols,
):
    depth, width, lateral = pressure.shape
    slabs = lax.axis_size("slab")
    columns = lax.axis_size("col")
    lines = depth * width
    grid = ((depth, width, lateral), F32)
    slots = slabs * 128
    nodes = columns * 128
    rows = mortar_blocks.shape[1]
    cells = nnc_cell[0, 0]
    faults = fault_cell[0, 0]
    blocks = mortar_blocks[0]
    tile_cols = mortar_cols[0]
    base = base_stress[0].reshape(3, rows, 128)
    slip0 = slip_start[0].reshape(3, rows, 128)
    stiff = stiff_diag[0].reshape(rows, 128)
    active = active_set[:, 0].reshape(-1, rows, 128)
    tiles = pltpu.VMEM((3, columns * rows, 128), F32)
    layer, wall = (width, lateral), (depth, lateral)
    table = pltpu.VMEM((lines, slots), BF16)
    block = pltpu.VMEM((depth, width, lateral), F32)
    packet = pltpu.VMEM((slabs, lateral, 128), BF16)
    values = pltpu.VMEM((2 * lateral, slots), BF16)
    edges = [((1, *layer), BF16)] * 2 + [((1, *wall), BF16)] * 2
    doubled = [((2, *layer), BF16)] * 2 + [((2, *wall), BF16)] * 2
    planes = 7 * rows

    outgoing, ready, cells, *sides = call(
        first_kernel,
        [
            ((slabs, lateral, 128), BF16, 0),
            ((1, 3 * rows, 128), BF16),
            (cells.shape, jnp.int32),
            *doubled,
        ],
        pressure,
        trans_z,
        trans_x,
        slip0,
        cells,
        hbm=(0, 1, 2, 3),
        scratch=(
            table,
            block,
            pltpu.VMEM((depth, 8, lateral), F32),
            pltpu.VMEM(layer, F32),
            pltpu.VMEM(slip0.shape, F32),
            packet,
            pltpu.SemaphoreType.DMA((4 + slabs // 2,)),
        ),
    )
    incoming = swap(outgoing, "slab")
    sides = exchange(sides)
    held = double(double(ready, "col", STEPS[0]), "col", STEPS[1])
    held, incoming, sides = lax.optimization_barrier((held, incoming, sides))
    faces = sides
    turned, diag = nnc_trans[0, 0], accum
    field = pressure
    for sweep in range(ITERS_FLOW):
        first = sweep == 0
        last = sweep == ITERS_FLOW - 1
        extra = [] if first else list(faces)
        if last:
            extra += [faults, own, fault_hot]
            outs = [
                (grid[0], F32),
                ((lines, nodes), BF16),
                ((columns, planes, 128), BF16),
            ]
        else:
            outs = [(*grid, 0), ((slabs, lateral, 128), BF16, 0)]
            if first:
                outs += [((slabs, lateral, 128), F32, 0), (*grid, 0)]
            outs += edges
        got = call(
            functools.partial(sweep_kernel, first, last),
            outs,
            incoming,
            turned,
            field,
            source,
            trans_z,
            trans_x,
            trans_y,
            diag,
            cells,
            *sides,
            *extra,
            hbm=(*range(1, 8), *([19] if last else [])),
            scratch=[
                *([] if last else [packet, block]),
                *([values] if first else []),
                *[block] * 6,
                pltpu.VMEM((slabs, lateral, 128), F32),
                values,
                table,
                pltpu.SemaphoreType.DMA((11 + slabs // 2,)),
            ],
        )
        if last:
            field, fault_hot, whole = got
            break
        field, outgoing = got[:2]
        if first:
            turned, diag = got[2:4]
            held, outgoing = lax.optimization_barrier((held, outgoing))
        else:
            held, other, outgoing = lax.optimization_barrier((held, other, outgoing))
        incoming = swap(outgoing, "slab")
        sides = exchange(got[-4:])
        if first:
            other = paired(held, "col", STEPS[2])
            other, incoming, sides = lax.optimization_barrier((other, incoming, sides))
        else:
            near = jnp.concatenate([held, other], 0)
            far = paired(near, "col", STEPS[3])
            own, fault_hot = call(
                functools.partial(contact_kernel, width),
                [((4 * rows, 128), F32), ((lines, nodes), BF16, 0)],
                tile_cols,
                near,
                far,
                blocks,
                base,
                slip0,
                stiff,
                active,
                faults,
                smem=(0,),
                hbm=(3,),
                scratch=(
                    tiles,
                    pltpu.VMEM(blocks.shape, BF16),
                    pltpu.VMEM((lines, nodes), BF16),
                    pltpu.SemaphoreType.DMA((2,)),
                ),
            )
    whole = swap(whole, "col")
    normal, slip, traction = call(
        tail_kernel,
        [((rows, 128), F32), ((3, rows, 128), F32), ((3, rows, 128), F32)],
        tile_cols,
        whole,
        blocks,
        base,
        own,
        stiff,
        active,
        smem=(0,),
        scratch=(pltpu.VMEM((columns * rows, 128), F32), tiles),
    )
    normal = swap(normal.reshape(columns, -1, 128), "col").reshape(columns, 128)
    (pressure_out,) = call(
        back_kernel,
        [grid],
        normal,
        faults,
        fault_hot,
        field,
        diag,
        scratch=(pltpu.VMEM((2 * lateral, nodes), BF16),),
    )
    return (pressure_out, slip.reshape(1, 3, -1), traction.reshape(1, 3, -1))


def solution(mesh):
    return jax.shard_map(
        per_device,
        mesh=mesh,
        in_specs=(
            P("slab", "col", None),
            P("slab", "col", None),
            P("slab", "col", None),
            P("slab", "col", None),
            P("slab", "col", None),
            P("slab", "col", None),
            P("slab", "col", None, None),
            P("slab", "col", None, None, None),
            P("slab", "col", None, None),
            P("slab", None, "col"),
            P("slab", None, "col"),
            P("slab", "col"),
            P(None, "slab", "col"),
            P("slab", "col", None, None, None),
            P("slab", "col", None),
        ),
        out_specs=(P("slab", "col", None), P("slab", None, "col"), P("slab", None, "col")),
        check_vma=False,
    )
```
